32 devices in a mesh: lev: 8 (over z, x), tile: 4 (over y, core).
Axes of the slice: x: 2, y: 2, z: 4, core: 2. Of those that a mesh axis runs over, the one named last changes fastest.
Arguments:
- increment: float32 [144, 96, 1440], P('lev', 'tile'), may hold values from -6 to 6
- kappa: float32 [144], P('lev'), may hold values from 0.02 to 0.24
- balance: float32 [144, 144], replicated, may hold values from -0.5 to 0.5
- correlation: float32 [144, 144], replicated, may hold values from -0.5 to 0.5
- ground_level: int32 [96, 1440], P('tile'), may hold values from 72 to 144
Outputs:
- covaried: float32 [144, 96, 1440], P('lev', 'tile')
The draws below stay inside these ranges and needn't reach their ends.
Inputs may be any that keep to these rules, and one draw needn't show every extreme that they name: Levels from ground_level of a column down to the last one lie below ground.
All inputs are finite; a program needn't handle non-finite values.
Results may differ from the reference program's by a relative error of at most 0.00019.
Values sent between devices are 32-bit elements; how exact they have to be, the bound alone decides.
No kernel may reach another device: no remote copies, remote signals or barrier semaphores. Data moves between devices by JAX's collectives and lax.ppermute only.
A program may use at most 64 MiB of HBM per device.

```python
import math
import jax
import jax.numpy as jnp
from jax import lax

LEVELS = 144
NLON = 1440
PASSES = 10
NLAT = 96


def set_ends(entries, rng, low, high):
    shape = entries.shape
    index_at = [jax.random.randint(jax.random.fold_in(rng, axis), (), 0, shape[axis]) for axis in range(len(shape))]
    entries = entries.at[tuple(index_at)].set(low)
    longest = shape.index(max(shape))
    index_at[longest] = (index_at[longest] + 1) % shape[longest]
    return entries.at[tuple(index_at)].set(high)


def level_of(stream_key, dims, cuts, least, largest):
    factor_of, own = 1.0, jax.random.fold_in(stream_key, 6)
    for dim, shards_of in cuts:
        draws = jnp.exp(jax.random.uniform(jax.random.fold_in(own, dim), (shards_of,), jnp.float32, least / len(cuts), largest / len(cuts)))
        factor_of = factor_of * jnp.repeat(draws, dims[dim] // shards_of).reshape([-1 if axis == dim else 1 for axis in range(len(dims))])
    return factor_of


def bell_draw(own_key, dims, width, reach, shards=(), held_as=jnp.bfloat16):
    values = width * jax.random.normal(own_key, dims, jnp.float32)
    if shards:
        values = values * level_of(own_key, dims, shards, -0.22, 0.18)
    return jnp.clip(values, -reach, reach).astype(held_as)


def setup_inputs(seed: int = 0) -> dict:
    arg_keys = jax.random.split(jax.random.key(seed), 6)
    increment = bell_draw(arg_keys[0], (LEVELS, NLAT, NLON), 1.0, 6.0, ((0, 8), (1, 4)), jnp.float32)
    kappa = jnp.clip(jnp.exp(math.log(0.24) - 2.4849066 * jax.random.uniform(arg_keys[1], (LEVELS,), jnp.float32) ** level_of(arg_keys[1], (LEVELS,), ((0, 8),), -0.2, 0.2)), 0.02, 0.24)
    balance = bell_draw(arg_keys[2], (LEVELS, LEVELS), LEVELS ** -0.5, 0.5, (), jnp.float32)
    correlation = bell_draw(arg_keys[3], (LEVELS, LEVELS), LEVELS ** -0.5, 0.5, (), jnp.float32)
    ground_level = set_ends(jax.random.randint(arg_keys[4], (NLAT, NLON), LEVELS // 2, LEVELS + 1), jax.random.fold_in(arg_keys[4], 1), LEVELS // 2, LEVELS).astype(jnp.int32)
    return dict(increment=increment, kappa=kappa, balance=balance, correlation=correlation, ground_level=ground_level)


def reference(increment, kappa, balance, correlation, ground_level):
    smoothed = increment
    diffusivity = kappa[:, None, None]
    for counter in range(PASSES):
        padded = jnp.pad(smoothed, ((0, 0), (1, 1), (0, 0)))
        beside = padded[:, 2:] + padded[:, :-2] + jnp.roll(smoothed, 1, 2) + jnp.roll(smoothed, -1, 2)
        smoothed = smoothed + diffusivity * (beside - 4.0 * smoothed)
    flattened = smoothed.reshape(LEVELS, NLAT * NLON)
    balanced = jnp.dot(balance, flattened, precision=lax.Precision.HIGHEST, preferred_element_type=jnp.float32)
    correlated = jnp.dot(correlation, balanced, precision=lax.Precision.HIGHEST, preferred_element_type=jnp.float32)
    level_index = lax.broadcasted_iota(jnp.int32, (LEVELS, 1), 0)
    above_ground = level_index < ground_level.reshape(1, NLAT * NLON).astype(jnp.int32)
    covaried = jnp.where(above_ground, correlated, jnp.zeros((), jnp.float32))
    return covaried.reshape(LEVELS, NLAT, NLON)
```

```python
import functools

import jax
import jax.numpy as jnp
import numpy as np
from jax import lax
from jax.experimental import pallas as pl
from jax.experimental.pallas import tpu as pltpu
from jax.sharding import PartitionSpec as P

PASSES = 10
LANES = 128
SUBS = 8

VMEM = pl.BlockSpec(memory_space=pltpu.VMEM)


def level_chunks(levels):
    chunks = [(first, SUBS) for first in range(0, levels - levels % SUBS, SUBS)]
    if levels % SUBS:
        chunks.append((levels - levels % SUBS, levels % SUBS))
    return chunks


def up_to(value, multiple):
    return -(-value // multiple) * multiple


class Plan:
    def __init__(self, shape, group):
        self.levels, self.rows, self.lons = shape
        self.group = group
        self.halo = PASSES
        self.full = self.lons // LANES
        self.rest = self.lons % LANES
        self.tiles = self.full + 1
        assert self.halo <= self.rest and self.rest + 2 * self.halo <= LANES
        assert self.halo <= self.rows and group & (group - 1) == 0
        self.rows_each = -(-self.rows // group)
        self.rows_held = self.rows_each * group
        self.per_merged = LANES // self.rest
        self.merged = -(-self.rows_each // self.per_merged)
        self.units = self.rows_each * self.full + self.merged
        self.chunks = level_chunks(self.levels)


def lane_ids():
    return lax.broadcasted_iota(jnp.int32, (SUBS, LANES), 1)


def arrange_kernel(plan, x_ref, *out_refs):
    lane = lane_ids()
    for (first, count), (all_ref, top_ref, bottom_ref) in zip(
        plan.chunks, zip(out_refs[0::3], out_refs[1::3], out_refs[2::3])
    ):
        for row in range(plan.rows):

            def take(tile):
                width = LANES if tile < plan.full else plan.rest
                value = x_ref[first : first + count, row, tile * LANES : tile * LANES + width]
                if count < SUBS or width < LANES:
                    value = jnp.pad(value, ((0, SUBS - count), (0, LANES - width)))
                return value

            values = [take(tile) for tile in range(plan.tiles)]
            last = values[-1]
            last = jnp.where(
                lane < plan.rest,
                last,
                jnp.where(
                    lane < plan.rest + plan.halo,
                    pltpu.roll(values[0], plan.rest, 1),
                    pltpu.roll(last, LANES - plan.rest, 1),
                ),
            )
            values[-1] = last
            for tile, value in enumerate(values):
                all_ref[row, tile] = value
                if row < plan.halo:
                    top_ref[row, tile] = value
                if row >= plan.rows - plan.halo:
                    bottom_ref[row - (plan.rows - plan.halo), tile] = value


def diffuse_kernel(plan, count, x_ref, before_ref, after_ref, kappa_ref, *refs):
    out_refs, (a_ref, b_ref) = refs[: plan.group], refs[plan.group :]
    me = lax.axis_index("lev")
    tile_index = lax.axis_index("tile")
    rows_total = plan.rows * lax.axis_size("tile")
    first_row = tile_index * plan.rows - plan.halo
    height = plan.rows + 2 * plan.halo
    lane = lane_ids()
    at_start, at_end = lane == 0, lane == LANES - 1
    kappa = kappa_ref[...]
    a_ref[: plan.halo] = before_ref[...]
    a_ref[plan.halo : plan.halo + plan.rows] = x_ref[...]
    a_ref[plan.halo + plan.rows : height] = after_ref[...]

    def sweep(source, target, done):
        def one_row(row, _):
            here = [source[row, tile] for tile in range(plan.tiles)]
            right = [pltpu.roll(value, 1, 1) for value in here]
            left = [pltpu.roll(value, LANES - 1, 1) for value in here]
            inside = (first_row + row >= 0) & (first_row + row < rows_total)
            weight = jnp.where(inside, kappa, 0.0)
            centre = 1.0 - 4.0 * weight
            for tile in range(plan.tiles):
                west = jnp.where(at_start, right[tile - 1], right[tile])
                east = jnp.where(at_end, left[(tile + 1) % plan.tiles], left[tile])
                beside = (source[row - 1, tile] + source[row + 1, tile]) + (west + east)
                target[row, tile] = centre * here[tile] + weight * beside
            return 0

        lax.fori_loop(done + 1, height - 1 - done, one_row, 0)

    def two_passes(step, _):
        sweep(a_ref, b_ref, 2 * step)
        sweep(b_ref, a_ref, 2 * step + 1)
        return 0

    lax.fori_loop(0, PASSES // 2, two_passes, 0)

    for d in range(plan.group):
        base = plan.halo + (me ^ d) * plan.rows_each

        def put(unit, value):
            if count == SUBS:
                out_refs[d][unit] = value
            else:
                out_refs[d][unit * count : (unit + 1) * count] = value[:count]

        for i in range(plan.rows_each):
            for tile in range(plan.full):
                put(i * plan.full + tile, a_ref[base + i, tile])
        for m in range(plan.merged):
            value = None
            for k in range(plan.per_merged):
                i = m * plan.per_merged + k
                if i < plan.rows_each:
                    piece = a_ref[base + i, plan.full]
                    if k == 0:
                        value = piece
                    else:
                        value = jnp.where(
                            lane < k * plan.rest, value, pltpu.roll(piece, k * plan.rest, 1)
                        )
            put(plan.rows_each * plan.full + m, value)


def mix_kernel(plan, first, stop, high_ref, low_ref, *refs):
    chunks, group, levels = plan.chunks, plan.group, plan.levels
    held = [refs[c * group : (c + 1) * group] for c in range(len(chunks))]
    out_refs = refs[len(chunks) * group : (len(chunks) + 1) * group]
    high, low = high_ref[...], low_ref[...]
    stride = up_to(levels, SUBS)
    for unit in range(first, stop):
        pieces = []
        for (_, count), blocks in zip(chunks, held):
            for block in blocks:
                if count == SUBS:
                    pieces.append(block[unit])
                else:
                    pieces.append(block[unit * count : (unit + 1) * count])
        column = jnp.concatenate(pieces, axis=0)
        column_high = column.astype(jnp.bfloat16)
        column_low = (column - column_high.astype(jnp.float32)).astype(jnp.bfloat16)

        def dot(matrix, values):
            return jnp.dot(matrix, values, preferred_element_type=jnp.float32)

        result = dot(high, column_high) + (dot(high, column_low) + dot(low, column_high))
        for d in range(group):
            out_refs[d][(unit - first) * levels : (unit - first + 1) * levels] = result[
                d * stride : d * stride + levels
            ]


def finish_kernel(plan, splits, ground_ref, *refs):
    group, levels = plan.group, plan.levels
    blocks = [refs[s * group : (s + 1) * group] for s in range(len(splits))]
    out_ref, held_ref = refs[len(splits) * group :]
    me = lax.axis_index("lev")
    rows_held = plan.rows_held

    def store(tile, row, value):
        for first in range(0, levels, SUBS):
            count = min(SUBS, levels - first)
            held_ref[tile, pl.ds(row + first * rows_held, count, stride=rows_held), :] = value[
                first : first + count
            ]

    for (begin, stop), received in zip(splits, blocks):
        for d in range(group):
            base = (me ^ d) * plan.rows_each
            for unit in range(begin, stop):
                value = received[d][(unit - begin) * levels : (unit - begin + 1) * levels]
                if unit < plan.rows_each * plan.full:
                    store(unit % plan.full, base + unit // plan.full, value)
                else:
                    m = unit - plan.rows_each * plan.full
                    for k in range(plan.per_merged):
                        i = m * plan.per_merged + k
                        if i < plan.rows_each:
                            piece = pltpu.roll(value, LANES - k * plan.rest, 1) if k else value
                            store(plan.full, base + i, piece)
    for tile in range(plan.tiles):
        width = LANES if tile < plan.full else plan.rest
        lanes = slice(tile * LANES, tile * LANES + width)
        ground = ground_ref[:, lanes]
        for level in range(levels):
            value = held_ref[tile, level * rows_held : level * rows_held + plan.rows, :width]
            out_ref[level, :, lanes] = jnp.where(me * levels + level < ground, value, 0.0)


def local(increment, kappa, balance, correlation, ground_level):
    group = lax.axis_size("lev")
    tiles_around = lax.axis_size("tile")
    plan = Plan(increment.shape, group)
    levels, halo = plan.levels, plan.halo
    me = lax.axis_index("lev")
    f32 = jnp.float32

    def shape(*dims):
        return jax.ShapeDtypeStruct(dims, f32)

    def call(kernel, outs, *, scratch=(), name, flops):
        return lambda *args: pl.pallas_call(
            kernel,
            out_shape=outs,
            in_specs=[VMEM] * len(args),
            out_specs=jax.tree.map(lambda _: VMEM, outs),
            scratch_shapes=list(scratch),
            name=name,
            compiler_params=pltpu.CompilerParams(vmem_limit_bytes=48 << 20),
            cost_estimate=pl.CostEstimate(flops=flops, bytes_accessed=1 << 20, transcendentals=0),
        )(*args)

    outs = []
    for _ in plan.chunks:
        outs += [shape(plan.rows, plan.tiles, SUBS, LANES)]
        outs += [shape(halo, plan.tiles, SUBS, LANES)] * 2
    arranged = call(
        functools.partial(arrange_kernel, plan), tuple(outs), name="arrange", flops=10**7
    )(increment)
    up = [(i, i + 1) for i in range(tiles_around - 1)]
    down = [(j, i) for i, j in up]
    halos = []
    for c in range(len(plan.chunks)):
        _, top, bottom = arranged[3 * c : 3 * c + 3]
        halos.append((lax.ppermute(bottom, "tile", up), lax.ppermute(top, "tile", down)))

    partner = me ^ np.arange(group, dtype=np.int32)
    stride = up_to(levels, SUBS)
    row_level = np.tile(np.arange(stride), group)
    row_of = jnp.where(
        row_level < levels, partner[np.arange(group * stride) // stride] * levels + row_level, -1
    )
    who, where = [], []
    for first, count in plan.chunks:
        for d in range(group):
            who += [d] * count
            where += list(range(first, first + count))
    column_of = partner[np.array(who)] * levels + np.array(where, np.int32)
    every = jnp.arange(group * levels, dtype=jnp.int32)
    exact = functools.partial(
        jnp.dot, precision=lax.Precision.HIGHEST, preferred_element_type=f32
    )
    left = exact((row_of[:, None] == every[None, :]).astype(f32), correlation)
    right = exact(balance, (every[:, None] == column_of[None, :]).astype(f32))
    operator = exact(left, right)
    high = operator.astype(jnp.bfloat16)
    low = (operator - high.astype(f32)).astype(jnp.bfloat16)

    def exchange(blocks):
        order = sorted(range(1, group), reverse=True)
        got = {0: blocks[0]}
        for d in order:
            got[d] = lax.ppermute(blocks[d], "lev", [(i, i ^ d) for i in range(group)])
        return [got[d] for d in range(group)]

    held = []
    for c, (first, count) in enumerate(plan.chunks):
        factor = jnp.pad(kappa[first : first + count], (0, SUBS - count))
        factor = jnp.broadcast_to(factor[:, None], (SUBS, LANES))
        if count == SUBS:
            block = shape(plan.units, SUBS, LANES)
        else:
            block = shape(up_to(plan.units * count, SUBS), LANES)
        height = plan.rows_held + 2 * halo
        blocks = call(
            functools.partial(diffuse_kernel, plan, count),
            (block,) * group,
            scratch=[pltpu.VMEM((height, plan.tiles, SUBS, LANES), f32)] * 2,
            name=f"diffuse_{c}",
            flops=10**9,
        )(arranged[3 * c], *halos[c], factor)
        held += exchange(blocks)

    middle = plan.units // 2
    splits = [(0, middle), (middle, plan.units)]
    back = []
    for s, (begin, stop) in enumerate(splits):
        block = shape(up_to((stop - begin) * levels, SUBS), LANES)
        blocks = call(
            functools.partial(mix_kernel, plan, begin, stop),
            (block,) * group,
            name=f"mix_{s}",
            flops=10**9,
        )(high, low, *held)
        back += exchange(blocks)

    return call(
        functools.partial(finish_kernel, plan, splits),
        shape(*increment.shape),
        scratch=[pltpu.VMEM((plan.tiles, levels * plan.rows_held, LANES), f32)],
        name="finish",
        flops=10**7,
    )(ground_level, *back)


def solution(mesh):
    return jax.shard_map(
        local,
        mesh=mesh,
        in_specs=(P("lev", "tile", None), P("lev"), P(), P(), P("tile", None)),
        out_specs=P("lev", "tile", None),
        check_vma=False,
    )
```

```python
import functools

import jax
import jax.numpy as jnp
import numpy as np
from jax import lax
from jax.experimental import pallas as pl
from jax.experimental.pallas import tpu as pltpu
from jax.sharding import PartitionSpec as P

PASSES = 10
LANES = 128
SUBS = 8
TOGETHER = 8

VMEM = pl.BlockSpec(memory_space=pltpu.VMEM)
ANY = pl.BlockSpec(memory_space=pl.ANY)


def level_chunks(levels):
    chunks = [(first, SUBS) for first in range(0, levels - levels % SUBS, SUBS)]
    if levels % SUBS:
        chunks.append((levels - levels % SUBS, levels % SUBS))
    return chunks


def up_to(value, multiple):
    return -(-value // multiple) * multiple


class Plan:
    def __init__(self, shape, group):
        self.levels, self.rows, self.lons = shape
        self.group = group
        self.halo = PASSES
        self.full = self.lons // LANES
        self.rest = self.lons % LANES
        self.tiles = self.full + 1
        assert self.halo <= self.rest and self.rest + 2 * self.halo <= LANES
        assert self.halo <= self.rows and group & (group - 1) == 0
        self.rows_each = -(-self.rows // group)
        self.rows_held = self.rows_each * group
        self.per_merged = LANES // self.rest
        self.merged = -(-self.rows_each // self.per_merged)
        self.units = self.rows_each * self.full + self.merged
        self.chunks = level_chunks(self.levels)


def lane_ids():
    return lax.broadcasted_iota(jnp.int32, (SUBS, LANES), 1)


def arrange_kernel(plan, chunks, x_ref, all_ref, top_ref, bottom_ref):
    lane = lane_ids()
    for c, (first, count) in enumerate(chunks):
        for row in range(plan.rows):

            def take(tile):
                width = LANES if tile < plan.full else plan.rest
                value = x_ref[first : first + count, row, tile * LANES : tile * LANES + width]
                if count < SUBS or width < LANES:
                    value = jnp.pad(value, ((0, SUBS - count), (0, LANES - width)))
                return value

            values = [take(tile) for tile in range(plan.tiles)]
            last = values[-1]
            values[-1] = jnp.where(
                lane < plan.rest,
                last,
                jnp.where(
                    lane < plan.rest + plan.halo,
                    pltpu.roll(values[0], plan.rest, 1),
                    pltpu.roll(last, LANES - plan.rest, 1),
                ),
            )
            for tile, value in enumerate(values):
                all_ref[c, row, tile] = value
                if row < plan.halo:
                    top_ref[c, row, tile] = value
                if row >= plan.rows - plan.halo:
                    bottom_ref[c, row - (plan.rows - plan.halo), tile] = value


def diffuse_kernel(plan, count, at, x_ref, before_ref, after_ref, kappa_ref, *refs):
    refs = refs[-plan.group - 2 :]
    out_refs, (a_ref, b_ref) = refs[: plan.group], refs[plan.group :]
    me = lax.axis_index("lev")
    tile_index = lax.axis_index("tile")
    rows_total = plan.rows * lax.axis_size("tile")
    first_row = tile_index * plan.rows - plan.halo
    height = plan.rows + 2 * plan.halo
    lane = lane_ids()
    at_start, at_end = lane == 0, lane == LANES - 1
    kappa = kappa_ref[...]
    a_ref[: plan.halo] = before_ref[at]
    a_ref[plan.halo : plan.halo + plan.rows] = x_ref[at]
    a_ref[plan.halo + plan.rows : height] = after_ref[at]

    def sweep(source, target, done):
        def one_row(row):
            here = [source[row, tile] for tile in range(plan.tiles)]
            right = [pltpu.roll(value, 1, 1) for value in here]
            left = [pltpu.roll(value, LANES - 1, 1) for value in here]
            inside = (first_row + row >= 0) & (first_row + row < rows_total)
            weight = jnp.where(inside, kappa, 0.0)
            centre = 1.0 - 4.0 * weight
            for tile in range(plan.tiles):
                west = jnp.where(at_start, right[tile - 1], right[tile])
                east = jnp.where(at_end, left[(tile + 1) % plan.tiles], left[tile])
                beside = (source[row - 1, tile] + source[row + 1, tile]) + (west + east)
                target[row, tile] = centre * here[tile] + weight * beside

        def some_rows(step, _):
            for i in range(TOGETHER):
                one_row(done + 1 + step * TOGETHER + i)
            return 0

        count = height - 2 - 2 * done
        lax.fori_loop(0, (count + TOGETHER - 1) // TOGETHER, some_rows, 0)

    def two_passes(step, _):
        sweep(a_ref, b_ref, 2 * step)
        sweep(b_ref, a_ref, 2 * step + 1)
        return 0

    lax.fori_loop(0, PASSES // 2, two_passes, 0)

    for d in range(plan.group):
        base = plan.halo + (me ^ d) * plan.rows_each

        def put(unit, value):
            if count == SUBS:
                out_refs[d][unit] = value
            else:
                out_refs[d][unit * count : (unit + 1) * count] = value[:count]

        for i in range(plan.rows_each):
            for tile in range(plan.full):
                put(i * plan.full + tile, a_ref[base + i, tile])
        for m in range(plan.merged):
            value = None
            for k in range(plan.per_merged):
                i = m * plan.per_merged + k
                if i < plan.rows_each:
                    piece = a_ref[base + i, plan.full]
                    if k == 0:
                        value = piece
                    else:
                        value = jnp.where(
                            lane < k * plan.rest, value, pltpu.roll(piece, k * plan.rest, 1)
                        )
            put(plan.rows_each * plan.full + m, value)


def mix_kernel(plan, first, stop, high_ref, low_ref, *refs):
    chunks, group, levels = plan.chunks, plan.group, plan.levels
    held = [refs[c * group : (c + 1) * group] for c in range(len(chunks))]
    out_refs = refs[len(chunks) * group : (len(chunks) + 1) * group]
    high, low = high_ref[...], low_ref[...]
    stride = up_to(levels, SUBS)
    for unit in range(first, stop):
        pieces = []
        for (_, count), blocks in zip(chunks, held):
            for block in blocks:
                if count == SUBS:
                    pieces.append(block[unit])
                else:
                    pieces.append(block[unit * count : (unit + 1) * count])
        column = jnp.concatenate(pieces, axis=0)
        column_high = column.astype(jnp.bfloat16)
        column_low = (column - column_high.astype(jnp.float32)).astype(jnp.bfloat16)

        def dot(matrix, values):
            return jnp.dot(matrix, values, preferred_element_type=jnp.float32)

        result = dot(high, column_high) + (dot(high, column_low) + dot(low, column_high))
        for d in range(group):
            out_refs[d][(unit - first) * levels : (unit - first + 1) * levels] = result[
                d * stride : d * stride + levels
            ]


def finish_kernel(plan, splits, ground_ref, *refs):
    group, levels = plan.group, plan.levels
    blocks = [refs[s * group : (s + 1) * group] for s in range(len(splits))]
    out_ref, held_ref = refs[len(splits) * group :]
    me = lax.axis_index("lev")
    rows_held = plan.rows_held

    def store(tile, row, value):
        for first in range(0, levels, SUBS):
            count = min(SUBS, levels - first)
            held_ref[tile, pl.ds(row + first * rows_held, count, stride=rows_held), :] = value[
                first : first + count
            ]

    for (begin, stop), received in zip(splits, blocks):
        for d in range(group):
            base = (me ^ d) * plan.rows_each
            for unit in range(begin, stop):
                value = received[d][(unit - begin) * levels : (unit - begin + 1) * levels]
                if unit < plan.rows_each * plan.full:
                    store(unit % plan.full, base + unit // plan.full, value)
                else:
                    m = unit - plan.rows_each * plan.full
                    for k in range(plan.per_merged):
                        i = m * plan.per_merged + k
                        if i < plan.rows_each:
                            piece = pltpu.roll(value, LANES - k * plan.rest, 1) if k else value
                            store(plan.full, base + i, piece)
    for tile in range(plan.tiles):
        width = LANES if tile < plan.full else plan.rest
        lanes = slice(tile * LANES, tile * LANES + width)
        ground = ground_ref[:, lanes]
        for level in range(levels):
            value = held_ref[tile, level * rows_held : level * rows_held + plan.rows, :width]
            out_ref[level, :, lanes] = jnp.where(me * levels + level < ground, value, 0.0)


def local(increment, kappa, balance, correlation, ground_level):
    group = lax.axis_size("lev")
    tiles_around = lax.axis_size("tile")
    plan = Plan(increment.shape, group)
    levels, halo = plan.levels, plan.halo
    me = lax.axis_index("lev")
    f32 = jnp.float32

    def shape(*dims):
        return jax.ShapeDtypeStruct(dims, f32)

    def call(kernel, outs, *, scratch=(), name, flops, loose=0):
        return lambda *args: pl.pallas_call(
            kernel,
            out_shape=outs,
            in_specs=[VMEM] * (len(args) - loose) + [ANY] * loose,
            out_specs=jax.tree.map(lambda _: VMEM, outs),
            scratch_shapes=list(scratch),
            name=name,
            compiler_params=pltpu.CompilerParams(vmem_limit_bytes=48 << 20),
            cost_estimate=pl.CostEstimate(flops=flops, bytes_accessed=1 << 20, transcendentals=0),
        )(*args)

    up = [(i, i + 1) for i in range(tiles_around - 1)]
    down = [(j, i) for i, j in up]
    parts = [plan.chunks[:1], plan.chunks[1:]]
    fields, halos = [], []
    for p, chunks in enumerate(parts):
        outs = [shape(len(chunks), plan.rows, plan.tiles, SUBS, LANES)]
        outs += [shape(len(chunks), halo, plan.tiles, SUBS, LANES)] * 2
        field, top, bottom = call(
            functools.partial(arrange_kernel, plan, chunks), tuple(outs), name=f"arrange_{p}", flops=10**7
        )(increment)
        before, after = lax.ppermute(bottom, "tile", up), lax.ppermute(top, "tile", down)
        for c in range(len(chunks)):
            fields.append((field, c))
            halos.append((before, after))

    stride = up_to(levels, SUBS)
    rows_of = lax.iota(jnp.int32, group * stride)
    row_of = jnp.where(
        rows_of % stride < levels, (me ^ (rows_of // stride)) * levels + rows_of % stride, -1
    )
    column_of = []
    for first, count in plan.chunks:
        met = lax.iota(jnp.int32, group * count)
        column_of.append((me ^ (met // count)) * levels + first + met % count)
    column_of = jnp.concatenate(column_of)
    every = jnp.arange(group * levels, dtype=jnp.int32)
    exact = functools.partial(
        jnp.dot, precision=lax.Precision.HIGHEST, preferred_element_type=f32
    )
    left = exact((row_of[:, None] == every[None, :]).astype(f32), correlation)
    right = exact(balance, (every[:, None] == column_of[None, :]).astype(f32))
    operator = exact(left, right)
    high = operator.astype(jnp.bfloat16)
    low = (operator - high.astype(f32)).astype(jnp.bfloat16)

    def exchange(blocks):
        order = sorted(range(1, group), reverse=True)
        got = {0: blocks[0]}
        for d in order:
            got[d] = lax.ppermute(blocks[d], "lev", [(i, i ^ d) for i in range(group)])
        return [got[d] for d in range(group)]

    held, token = [], ()
    for c, (first, count) in enumerate(plan.chunks):
        factor = jnp.pad(kappa[first : first + count], (0, SUBS - count))
        factor = jnp.broadcast_to(factor[:, None], (SUBS, LANES))
        if count == SUBS:
            block = shape(plan.units, SUBS, LANES)
        else:
            block = shape(up_to(plan.units * count, SUBS), LANES)
        height = plan.rows_held + 2 * halo + TOGETHER
        blocks = call(
            functools.partial(diffuse_kernel, plan, count, fields[c][1]),
            (block,) * group,
            scratch=[pltpu.VMEM((height, plan.tiles, SUBS, LANES), f32)] * 2,
            name=f"diffuse_{c}",
            flops=10**9,
            loose=len(token),
        )(fields[c][0], *halos[c], factor, *token)
        token = blocks[:1]
        held += exchange(blocks)

    middle = plan.units // 2
    splits = [(0, middle), (middle, plan.units)]
    back = []
    for s, (begin, stop) in enumerate(splits):
        block = shape(up_to((stop - begin) * levels, SUBS), LANES)
        blocks = call(
            functools.partial(mix_kernel, plan, begin, stop),
            (block,) * group,
            name=f"mix_{s}",
            flops=10**9,
        )(high, low, *held)
        back += exchange(blocks)

    return call(
        functools.partial(finish_kernel, plan, splits),
        shape(*increment.shape),
        scratch=[pltpu.VMEM((plan.tiles, levels * plan.rows_held, LANES), f32)],
        name="finish",
        flops=10**7,
    )(ground_level, *back)


def solution(mesh):
    return jax.shard_map(
        local,
        mesh=mesh,
        in_specs=(P("lev", "tile", None), P("lev"), P(), P(), P("tile", None)),
        out_specs=P("lev", "tile", None),
        check_vma=False,
    )
```

```python
import functools

import jax
import jax.numpy as jnp
from jax import lax
from jax.experimental import pallas as pl
from jax.experimental.pallas import tpu as pltpu
from jax.sharding import PartitionSpec as P


PASSES = 10
LANES = 128
SUBS = 8
TOGETHER = 8
TOGETHER_CHUNKS = ()

VMEM = pl.BlockSpec(memory_space=pltpu.VMEM)
ANY = pl.BlockSpec(memory_space=pl.ANY)


def level_chunks(levels):
    chunks = [(first, SUBS) for first in range(0, levels - levels % SUBS, SUBS)]
    if levels % SUBS:
        chunks.append((levels - levels % SUBS, levels % SUBS))
    return chunks


def up_to(value, multiple):
    return -(-value // multiple) * multiple


class Plan:
    def __init__(self, shape, group):
        self.levels, self.rows, self.lons = shape
        self.group = group
        self.halo = PASSES
        self.full = self.lons // LANES
        self.rest = self.lons % LANES
        self.tiles = self.full + 1
        assert self.halo <= self.rest and self.rest + 2 * self.halo <= LANES
        assert self.halo <= self.rows and group & (group - 1) == 0
        self.rows_each = -(-self.rows // group)
        self.rows_held = self.rows_each * group
        self.per_merged = LANES // self.rest
        self.merged = -(-self.rows_each // self.per_merged)
        self.units = self.rows_each * self.full + self.merged
        self.chunks = level_chunks(self.levels)


def lane_ids():
    return lax.broadcasted_iota(jnp.int32, (SUBS, LANES), 1)


def arrange_kernel(plan, chunks, x_ref, all_ref, inner_ref, outer_ref, x_vmem, sem):
    begin = chunks[0][0]
    levels = chunks[-1][0] + chunks[-1][1] - begin
    copy = pltpu.make_async_copy(x_ref.at[begin : begin + levels], x_vmem, sem)
    copy.start()
    copy.wait()
    lane = lane_ids()
    even = lax.axis_index("tile") % 2 == 0
    inner_row = jnp.where(even, plan.rows - plan.halo, 0)
    outer_row = jnp.where(even, 0, plan.rows - plan.halo)
    for c, (first, count) in enumerate(chunks):
        for row in range(plan.rows):

            def take(tile):
                width = LANES if tile < plan.full else plan.rest
                lanes = slice(tile * LANES, tile * LANES + width)
                value = x_vmem[first - begin : first - begin + count, row, lanes]
                if count < SUBS or width < LANES:
                    value = jnp.pad(value, ((0, SUBS - count), (0, LANES - width)))
                return value

            values = [take(tile) for tile in range(plan.tiles)]
            last = values[-1]
            values[-1] = jnp.where(
                lane < plan.rest,
                last,
                jnp.where(
                    lane < plan.rest + plan.halo,
                    pltpu.roll(values[0], plan.rest, 1),
                    pltpu.roll(last, LANES - plan.rest, 1),
                ),
            )
            for tile, value in enumerate(values):
                all_ref[c, row, tile] = value
        for row in range(plan.halo):
            for tile in range(plan.tiles):
                inner_ref[c, row, tile] = all_ref[c, inner_row + row, tile]
                outer_ref[c, row, tile] = all_ref[c, outer_row + row, tile]


def diffuse_kernel(plan, count, at, together, x_ref, inner_ref, outer_ref, kappa_ref, *refs):
    out_refs, (a_ref, b_ref) = refs[:-2], refs[-2:]
    me = lax.axis_index("lev")
    tile_index = lax.axis_index("tile")
    rows_total = plan.rows * lax.axis_size("tile")
    first_row = tile_index * plan.rows - plan.halo
    height = plan.rows + 2 * plan.halo
    lane = lane_ids()
    at_start, at_end = lane == 0, lane == LANES - 1
    kappa = kappa_ref[...]
    below = plan.halo + plan.rows
    inner_row = jnp.where(tile_index % 2 == 0, below, 0)
    for row in range(plan.halo):
        a_ref[inner_row + row] = inner_ref[at, row]
        a_ref[below - inner_row + row] = outer_ref[at, row]
    a_ref[plan.halo : below] = x_ref[at]

    def sweep(source, target, done):
        def one_row(row):
            here = [source[row, tile] for tile in range(plan.tiles)]
            right = [pltpu.roll(value, 1, 1) for value in here]
            left = [pltpu.roll(value, LANES - 1, 1) for value in here]
            inside = (first_row + row >= 0) & (first_row + row < rows_total)
            weight = jnp.where(inside, kappa, 0.0)
            centre = 1.0 - 4.0 * weight
            for tile in range(plan.tiles):
                west = jnp.where(at_start, right[tile - 1], right[tile])
                east = jnp.where(at_end, left[(tile + 1) % plan.tiles], left[tile])
                beside = (source[row - 1, tile] + source[row + 1, tile]) + (west + east)
                target[row, tile] = centre * here[tile] + weight * beside

        def some_rows(step, _):
            for i in range(TOGETHER):
                one_row(done + 1 + step * TOGETHER + i)
            return 0

        count = height - 2 - 2 * done
        lax.fori_loop(0, (count + TOGETHER - 1) // TOGETHER, some_rows, 0)

    def two_passes(step, _):
        sweep(a_ref, b_ref, 2 * step)
        sweep(b_ref, a_ref, 2 * step + 1)
        return 0

    lax.fori_loop(0, PASSES // 2, two_passes, 0)

    for d in range(plan.group):
        out_ref = out_refs[0].at[d] if together else out_refs[d]
        base = plan.halo + (d if together else me ^ d) * plan.rows_each

        def put(unit, value):
            if count == SUBS:
                out_ref[unit] = value
            else:
                out_ref[unit * count : (unit + 1) * count] = value[:count]

        for i in range(plan.rows_each):
            for tile in range(plan.full):
                put(i * plan.full + tile, a_ref[base + i, tile])
        for m in range(plan.merged):
            value = None
            for k in range(plan.per_merged):
                i = m * plan.per_merged + k
                if i < plan.rows_each:
                    piece = a_ref[base + i, plan.full]
                    if k == 0:
                        value = piece
                    else:
                        value = jnp.where(
                            lane < k * plan.rest, value, pltpu.roll(piece, k * plan.rest, 1)
                        )
            put(plan.rows_each * plan.full + m, value)


def operator_kernel(plan, together, correlation_ref, balance_ref, high_ref, low_ref):
    group, levels = plan.group, plan.levels
    stride = up_to(levels, SUBS)
    me = lax.axis_index("lev")

    def exact(left, right, dims=((1,), (0,))):
        return lax.dot_general(
            left,
            right,
            (dims, ((), ())),
            precision=lax.Precision.HIGHEST,
            preferred_element_type=jnp.float32,
        )

    def picked(shape, pieces):
        place = lax.broadcasted_iota(jnp.int32, shape, 0)
        level = jnp.full(shape, -1, jnp.int32)
        for first, count, start in pieces:
            here = (place >= first) & (place < first + count)
            level = jnp.where(here, start + place - first, level)
        return (level == lax.broadcasted_iota(jnp.int32, shape, 1)).astype(jnp.float32)

    rows = [(d * stride, levels, (me ^ d) * levels) for d in range(group)]
    columns, place = [], 0
    for (first, count), alike in zip(plan.chunks, together):
        for d in range(group):
            columns.append((place, count, (d if alike else me ^ d) * levels + first))
            place += count
    left = exact(picked((group * stride, group * levels), rows), correlation_ref[...])
    right = exact(
        balance_ref[...], picked((group * levels, group * levels), columns), ((1,), (1,))
    )
    operator = exact(left, right)
    high = operator.astype(jnp.bfloat16)
    high_ref[...] = high
    low_ref[...] = (operator - high.astype(jnp.float32)).astype(jnp.bfloat16)


def mix_kernel(plan, counts, first, stop, high_ref, low_ref, *refs):
    chunks, group, levels = plan.chunks, plan.group, plan.levels
    held, place = [], 0
    for given in counts:
        refs_here = refs[place : place + given]
        held.append([refs_here[0].at[d] for d in range(group)] if given == 1 else refs_here)
        place += given
    out_refs = refs[place : place + group]
    high, low = high_ref[...], low_ref[...]
    stride = up_to(levels, SUBS)
    for unit in range(first, stop):
        pieces = []
        for (_, count), blocks in zip(chunks, held):
            for block in blocks:
                if count == SUBS:
                    pieces.append(block[unit])
                else:
                    pieces.append(block[unit * count : (unit + 1) * count])
        column = jnp.concatenate(pieces, axis=0)
        column_high = column.astype(jnp.bfloat16)
        column_low = (column - column_high.astype(jnp.float32)).astype(jnp.bfloat16)

        def dot(matrix, values):
            return jnp.dot(matrix, values, preferred_element_type=jnp.float32)

        result = dot(high, column_high) + (dot(high, column_low) + dot(low, column_high))
        for d in range(group):
            out_refs[d][(unit - first) * levels : (unit - first + 1) * levels] = result[
                d * stride : d * stride + levels
            ]


def unpack(plan, begin, stop, received, held_ref):
    levels, rows_held = plan.levels, plan.rows_held
    me = lax.axis_index("lev")

    def store(tile, row, value):
        for first in range(0, levels, SUBS):
            count = min(SUBS, levels - first)
            held_ref[tile, pl.ds(row + first * rows_held, count, stride=rows_held), :] = value[
                first : first + count
            ]

    for d in range(plan.group):
        base = (me ^ d) * plan.rows_each
        for unit in range(begin, stop):
            value = received[d][(unit - begin) * levels : (unit - begin + 1) * levels]
            if unit < plan.rows_each * plan.full:
                store(unit % plan.full, base + unit // plan.full, value)
            else:
                m = unit - plan.rows_each * plan.full
                for k in range(plan.per_merged):
                    i = m * plan.per_merged + k
                    if i < plan.rows_each:
                        piece = pltpu.roll(value, LANES - k * plan.rest, 1) if k else value
                        store(plan.full, base + i, piece)


def unpack_kernel(plan, begin, stop, *refs):
    unpack(plan, begin, stop, refs[:-1], refs[-1])


def finish_kernel(plan, begin, stop, ground_ref, held_ref, *refs):
    out_ref = refs[plan.group]
    levels, rows_held = plan.levels, plan.rows_held
    unpack(plan, begin, stop, refs[: plan.group], held_ref)
    me = lax.axis_index("lev")
    for tile in range(plan.tiles):
        width = LANES if tile < plan.full else plan.rest
        lanes = slice(tile * LANES, tile * LANES + width)
        ground = ground_ref[:, lanes]
        for level in range(levels):
            value = held_ref[tile, level * rows_held : level * rows_held + plan.rows, :width]
            out_ref[level, :, lanes] = jnp.where(me * levels + level < ground, value, 0.0)


def program(increment, kappa, balance, correlation, ground_level):
    group = lax.axis_size("lev")
    tiles_around = lax.axis_size("tile")
    plan = Plan(increment.shape, group)
    levels, halo = plan.levels, plan.halo
    f32 = jnp.float32

    def shape(*dims):
        return jax.ShapeDtypeStruct(dims, f32)

    def call(kernel, outs, *args, scratch=(), flops, first_spec=VMEM, aliases=None):
        return pl.pallas_call(
            kernel,
            out_shape=outs,
            in_specs=[first_spec] + [VMEM] * (len(args) - 1),
            out_specs=jax.tree.map(lambda _: VMEM, outs),
            scratch_shapes=list(scratch),
            input_output_aliases=aliases or {},
            compiler_params=pltpu.CompilerParams(vmem_limit_bytes=14 << 20),
            cost_estimate=pl.CostEstimate(flops=flops, bytes_accessed=1 << 20, transcendentals=0),
        )(*args)

    def swap(start):
        return [(i + k, i + 1 - k) for i in range(start, tiles_around - 1, 2) for k in range(2)]

    parts = [plan.chunks[:1], plan.chunks[1:]]
    fields = []
    for chunks in parts:
        held_levels = sum(count for _, count in chunks)
        field = shape(len(chunks), plan.rows, plan.tiles, SUBS, LANES)
        edge = shape(len(chunks), halo, plan.tiles, SUBS, LANES)
        field, inner, outer = call(
            functools.partial(arrange_kernel, plan, chunks),
            (field, edge, edge),
            increment,
            scratch=[
                pltpu.VMEM((held_levels, *increment.shape[1:]), f32),
                pltpu.SemaphoreType.DMA,
            ],
            flops=10**7,
            first_spec=pl.BlockSpec(memory_space=pltpu.HBM),
        )
        outer = lax.ppermute(outer, "tile", swap(1))
        inner = lax.ppermute(inner, "tile", swap(0))
        fields += [(c, field, inner, outer) for c in range(len(chunks))]

    def exchange(blocks):
        if not isinstance(blocks, tuple):
            return [lax.all_to_all(blocks, "lev", 0, 0, tiled=True)]
        got = {0: blocks[0]}
        for d in reversed(range(1, group)):
            got[d] = lax.ppermute(blocks[d], "lev", [(i, i ^ d) for i in range(group)])
        return [got[d] for d in range(group)]

    together = [c in TOGETHER_CHUNKS for c in range(len(plan.chunks))]
    held, counts = [], []
    for c, (first, count) in enumerate(plan.chunks):
        factor = jnp.pad(kappa[first : first + count], (0, SUBS - count))
        factor = jnp.broadcast_to(factor[:, None], (SUBS, LANES))
        if count == SUBS:
            block = (plan.units, SUBS, LANES)
        else:
            block = (up_to(plan.units * count, SUBS), LANES)
        height = plan.rows_held + 2 * halo + TOGETHER
        blocks = call(
            functools.partial(diffuse_kernel, plan, count, fields[c][0], together[c]),
            shape(group, *block) if together[c] else (shape(*block),) * group,
            *fields[c][1:],
            factor,
            scratch=[pltpu.VMEM((height, plan.tiles, SUBS, LANES), f32)] * 2,
            flops=10**9,
        )
        got = exchange(blocks)
        counts.append(len(got))
        held += got

    stride = up_to(levels, SUBS)
    operator = jax.ShapeDtypeStruct((group * stride, group * levels), jnp.bfloat16)
    high, low = call(
        functools.partial(operator_kernel, plan, together),
        (operator, operator),
        correlation,
        balance,
        flops=10**8,
    )

    half = plan.units // 2
    splits = [(0, half), (half, plan.units)]
    back = []
    for begin, stop in splits:
        block = shape(up_to((stop - begin) * levels, SUBS), LANES)
        blocks = call(
            functools.partial(mix_kernel, plan, counts, begin, stop),
            (block,) * group,
            high,
            low,
            *held,
            flops=10**9,
        )
        back.append(exchange(blocks))

    partly = call(
        functools.partial(unpack_kernel, plan, *splits[0]),
        shape(plan.tiles, levels * plan.rows_held, LANES),
        *back[0],
        flops=10**7,
    )
    return call(
        functools.partial(finish_kernel, plan, *splits[1]),
        shape(*increment.shape),
        ground_level,
        partly,
        *back[1],
        flops=10**7,
    )


def solution(mesh):
    return jax.shard_map(
        program,
        mesh=mesh,
        in_specs=(P("lev", "tile", None), P("lev"), P(), P(), P("tile", None)),
        out_specs=P("lev", "tile", None),
        check_vma=False,
    )
```

```python
import functools

import jax
import jax.numpy as jnp
from jax import lax
from jax.experimental import pallas as pl
from jax.experimental.pallas import tpu as pltpu
from jax.sharding import PartitionSpec as P


PASSES = 10
LANES = 128
SUBS = 8
UNROLLS = (4, 2)
DEAL = 4
TOGETHER_CHUNKS = ()

VMEM = pl.BlockSpec(memory_space=pltpu.VMEM)
ANY = pl.BlockSpec(memory_space=pl.ANY)


def level_chunks(levels):
    chunks = [(first, SUBS) for first in range(0, levels - levels % SUBS, SUBS)]
    if levels % SUBS:
        chunks.append((levels - levels % SUBS, levels % SUBS))
    return chunks


def up_to(value, multiple):
    return -(-value // multiple) * multiple


class Plan:
    def __init__(self, shape, group):
        self.levels, self.rows, self.lons = shape
        self.group = group
        self.halo = PASSES
        self.full = self.lons // LANES
        self.rest = self.lons % LANES
        self.tiles = self.full + 1
        assert self.halo <= self.rest and self.rest + 2 * self.halo <= LANES
        assert PASSES % 2 == 0 and self.tiles % DEAL == 0 and self.rows % 2 == 0
        assert self.halo <= self.rows and group & (group - 1) == 0
        self.rows_each = -(-self.rows // group)
        self.rows_held = self.rows_each * group
        self.per_merged = LANES // self.rest
        self.merged = -(-self.rows_each // self.per_merged)
        self.units = self.rows_each * self.full + self.merged
        self.chunks = level_chunks(self.levels)


def lane_ids():
    return lax.broadcasted_iota(jnp.int32, (SUBS, LANES), 1)


def swapped(tiles):
    lane = lane_ids()
    even, low = (lane & 32) == 0, lane < 64
    a, b, c, d = tiles
    first, second = (
        (jnp.where(even, x, pltpu.roll(y, 32, 1)), jnp.where(even, pltpu.roll(x, 96, 1), y))
        for x, y in ((a, b), (c, d))
    )
    (a, b), (c, d) = first, second
    return [
        jnp.where(low, a, pltpu.roll(c, 64, 1)),
        jnp.where(low, b, pltpu.roll(d, 64, 1)),
        jnp.where(low, pltpu.roll(a, 64, 1), c),
        jnp.where(low, pltpu.roll(b, 64, 1), d),
    ]


def lanes_taken(value, index):
    return jnp.take_along_axis(value, index, axis=1, mode="promise_in_bounds")


def dealt(tiles):
    lane = lane_ids()
    index = 4 * (lane & 31) + (lane >> 5)
    return swapped([lanes_taken(tile, index) for tile in tiles])


def gathered(tiles):
    lane = lane_ids()
    index = 32 * (lane & 3) + (lane >> 2)
    return [lanes_taken(tile, index) for tile in swapped(tiles)]


def arrange_kernel(plan, chunks, alone, x_ref, all_ref, inner_ref, outer_ref):
    begin = chunks[0][0] if alone else 0
    lane = lane_ids()
    even = lax.axis_index("tile") % 2 == 0
    inner_row = jnp.where(even, plan.rows - plan.halo, 0)
    outer_row = jnp.where(even, 0, plan.rows - plan.halo)
    for c, (first, count) in enumerate(chunks):
        for row in range(plan.rows):

            def take(tile):
                width = LANES if tile < plan.full else plan.rest
                lanes = slice(tile * LANES, tile * LANES + width)
                value = x_ref[first - begin : first - begin + count, row, lanes]
                if count < SUBS or width < LANES:
                    value = jnp.pad(value, ((0, SUBS - count), (0, LANES - width)))
                return value

            values = [take(tile) for tile in range(plan.tiles)]
            last = values[-1]
            values[-1] = jnp.where(
                lane < plan.rest,
                last,
                jnp.where(
                    lane < plan.rest + plan.halo,
                    pltpu.roll(values[0], plan.rest, 1),
                    pltpu.roll(last, LANES - plan.rest, 1),
                ),
            )
            for tile, value in enumerate(values):
                all_ref[c, row, tile] = value

        unroll = next(u for u in UNROLLS if plan.rows % u == 0)

        def deal(step, _):
            for i in range(unroll):
                row = step * unroll + i
                for tile in range(0, plan.tiles, DEAL):
                    values = [all_ref[c, row, tile + b] for b in range(DEAL)]
                    for b, value in enumerate(dealt(values)):
                        all_ref[c, row, tile + b] = value
            return 0

        lax.fori_loop(0, plan.rows // unroll, deal, 0)
        for row in range(plan.halo):
            for tile in range(plan.tiles):
                inner_ref[c, row, tile] = all_ref[c, inner_row + row, tile]
                outer_ref[c, row, tile] = all_ref[c, outer_row + row, tile]


def diffuse_kernel(plan, count, at, together, x_ref, inner_ref, outer_ref, kappa_ref, *refs):
    out_refs, (a_ref, b_ref) = refs[:-2], refs[-2:]
    me = lax.axis_index("lev")
    tile_index = lax.axis_index("tile")
    height = plan.rows + 2 * plan.halo
    lane = lane_ids()
    at_start, at_end = lane == 0, lane == LANES - 1
    kappa = kappa_ref[...]
    ratio = (1.0 - 4.0 * kappa) / kappa
    kept = {
        plan.halo - 1: jnp.where(tile_index == 0, 0.0, 1.0),
        plan.halo + plan.rows: jnp.where(tile_index == lax.axis_size("tile") - 1, 0.0, 1.0),
    }
    below = plan.halo + plan.rows
    inner_row = jnp.where(tile_index % 2 == 0, below, 0)
    for row in range(plan.halo):
        a_ref[inner_row + row] = inner_ref[at, row]
        a_ref[below - inner_row + row] = outer_ref[at, row]
    a_ref[plan.halo : below] = x_ref[at]

    groups = range(0, plan.tiles, DEAL)

    def sweep(source, target, first, stop):
        def turned(row):
            left = [pltpu.roll(source[row, t], LANES - 1, 1) for t in groups]
            right = [pltpu.roll(source[row, t + DEAL - 1], 1, 1) for t in groups]
            return left, right

        ahead = turned(first)
        for row in range(first, stop):
            left, right = ahead
            if row + 1 < stop:
                ahead = turned(row + 1)
            here = [source[row, tile] for tile in range(plan.tiles)]
            for tile in range(plan.tiles):
                g = tile // DEAL
                if tile % DEAL == 0:
                    west = jnp.where(at_start, right[g - 1], right[g])
                else:
                    west = here[tile - 1]
                if tile % DEAL == DEAL - 1:
                    east = jnp.where(at_end, left[(g + 1) % len(groups)], left[g])
                else:
                    east = here[tile + 1]
                beside = (source[row - 1, tile] + source[row + 1, tile]) + (west + east)
                value = ratio * here[tile] + beside
                target[row, tile] = value * kept[row] if row in kept else value

    def two_passes(done):
        def body(step, _):
            sweep(a_ref, b_ref, done + 1, height - 1 - done)
            sweep(b_ref, a_ref, done + 2, height - 2 - done)
            return 0

        return body

    early = PASSES // 4
    lax.fori_loop(0, early, two_passes(0), 0)
    lax.fori_loop(early, PASSES // 2, two_passes(2 * early), 0)
    power = kappa
    for _ in range(PASSES - 1):
        power = power * kappa

    unroll = next(u for u in UNROLLS if plan.rows % u == 0)

    def undo(step, _):
        for i in range(unroll):
            row = step * unroll + i
            for tile in groups:
                values = [a_ref[plan.halo + row, tile + b] * power for b in range(DEAL)]
                for b, value in enumerate(gathered(values)):
                    b_ref[row, tile + b] = value
        return 0

    lax.fori_loop(0, plan.rows // unroll, undo, 0)

    for d in range(plan.group):
        out_ref = out_refs[0].at[d] if together else out_refs[d]
        base = (d if together else me ^ d) * plan.rows_each

        def put(unit, value):
            if count == SUBS:
                out_ref[unit] = value
            else:
                out_ref[unit * count : (unit + 1) * count] = value[:count]

        for i in range(plan.rows_each):
            for tile in range(plan.full):
                put(i * plan.full + tile, b_ref[base + i, tile])
        for m in range(plan.merged):
            value = None
            for k in range(plan.per_merged):
                i = m * plan.per_merged + k
                if i < plan.rows_each:
                    piece = b_ref[base + i, plan.full]
                    if k == 0:
                        value = piece
                    else:
                        value = jnp.where(
                            lane < k * plan.rest, value, pltpu.roll(piece, k * plan.rest, 1)
                        )
            put(plan.rows_each * plan.full + m, value)


def operator_kernel(plan, together, correlation_ref, balance_ref, high_ref, low_ref):
    group, levels = plan.group, plan.levels
    stride = up_to(levels, SUBS)
    me = lax.axis_index("lev")

    def exact(left, right, dims=((1,), (0,))):
        return lax.dot_general(
            left,
            right,
            (dims, ((), ())),
            precision=lax.Precision.HIGHEST,
            preferred_element_type=jnp.float32,
        )

    def picked(shape, pieces):
        place = lax.broadcasted_iota(jnp.int32, shape, 0)
        level = jnp.full(shape, -1, jnp.int32)
        for first, count, start in pieces:
            here = (place >= first) & (place < first + count)
            level = jnp.where(here, start + place - first, level)
        return (level == lax.broadcasted_iota(jnp.int32, shape, 1)).astype(jnp.float32)

    rows = [(d * stride, levels, (me ^ d) * levels) for d in range(group)]
    columns, place = [], 0
    for (first, count), alike in zip(plan.chunks, together):
        for d in range(group):
            columns.append((place, count, (d if alike else me ^ d) * levels + first))
            place += count
    left = exact(picked((group * stride, group * levels), rows), correlation_ref[...])
    right = exact(
        balance_ref[...], picked((group * levels, group * levels), columns), ((1,), (1,))
    )
    operator = exact(left, right)
    high = operator.astype(jnp.bfloat16)
    high_ref[...] = high
    low_ref[...] = (operator - high.astype(jnp.float32)).astype(jnp.bfloat16)


def mix_kernel(plan, counts, first, stop, high_ref, low_ref, *refs):
    chunks, group, levels = plan.chunks, plan.group, plan.levels
    held, place = [], 0
    for given in counts:
        refs_here = refs[place : place + given]
        held.append([refs_here[0].at[d] for d in range(group)] if given == 1 else refs_here)
        place += given
    out_refs = refs[place : place + group]
    high, low = high_ref[...], low_ref[...]
    stride = up_to(levels, SUBS)
    for unit in range(first, stop):
        pieces = []
        for (_, count), blocks in zip(chunks, held):
            for block in blocks:
                if count == SUBS:
                    pieces.append(block[unit])
                else:
                    pieces.append(block[unit * count : (unit + 1) * count])
        column = jnp.concatenate(pieces, axis=0)
        column_high = column.astype(jnp.bfloat16)
        column_low = (column - column_high.astype(jnp.float32)).astype(jnp.bfloat16)

        def dot(matrix, values):
            return jnp.dot(matrix, values, preferred_element_type=jnp.float32)

        result = dot(high, column_high) + (dot(high, column_low) + dot(low, column_high))
        for d in range(group):
            out_refs[d][(unit - first) * levels : (unit - first + 1) * levels] = result[
                d * stride : d * stride + levels
            ]


def unpack(plan, begin, stop, received, held_ref):
    levels, rows_held = plan.levels, plan.rows_held
    me = lax.axis_index("lev")

    def store(tile, row, value):
        for first in range(0, levels, SUBS):
            count = min(SUBS, levels - first)
            held_ref[tile, pl.ds(row + first * rows_held, count, stride=rows_held), :] = value[
                first : first + count
            ]

    for d in range(plan.group):
        base = (me ^ d) * plan.rows_each
        for unit in range(begin, stop):
            value = received[d][(unit - begin) * levels : (unit - begin + 1) * levels]
            if unit < plan.rows_each * plan.full:
                store(unit % plan.full, base + unit // plan.full, value)
            else:
                m = unit - plan.rows_each * plan.full
                for k in range(plan.per_merged):
                    i = m * plan.per_merged + k
                    if i < plan.rows_each:
                        piece = pltpu.roll(value, LANES - k * plan.rest, 1) if k else value
                        store(plan.full, base + i, piece)


def unpack_kernel(plan, begin, stop, *refs):
    unpack(plan, begin, stop, refs[:-1], refs[-1])


def finish_kernel(plan, begin, stop, ground_ref, held_ref, *refs):
    out_ref = refs[plan.group]
    levels, rows_held = plan.levels, plan.rows_held
    unpack(plan, begin, stop, refs[: plan.group], held_ref)
    me = lax.axis_index("lev")
    for tile in range(plan.tiles):
        width = LANES if tile < plan.full else plan.rest
        lanes = slice(tile * LANES, tile * LANES + width)
        ground = ground_ref[:, lanes]
        for level in range(levels):
            value = held_ref[tile, level * rows_held : level * rows_held + plan.rows, :width]
            out_ref[level, :, lanes] = jnp.where(me * levels + level < ground, value, 0.0)


def program(increment, kappa, balance, correlation, ground_level):
    group = lax.axis_size("lev")
    tiles_around = lax.axis_size("tile")
    plan = Plan(increment.shape, group)
    levels, halo = plan.levels, plan.halo
    f32 = jnp.float32

    def shape(*dims):
        return jax.ShapeDtypeStruct(dims, f32)

    def call(kernel, outs, *args, scratch=(), flops, vmem=14 << 20):
        return pl.pallas_call(
            kernel,
            out_shape=outs,
            in_specs=[VMEM] * len(args),
            out_specs=jax.tree.map(lambda _: VMEM, outs),
            scratch_shapes=list(scratch),
            compiler_params=pltpu.CompilerParams(vmem_limit_bytes=vmem),
            cost_estimate=pl.CostEstimate(flops=flops, bytes_accessed=1 << 20, transcendentals=0),
        )(*args)

    def swap(start):
        return [(i + k, i + 1 - k) for i in range(start, tiles_around - 1, 2) for k in range(2)]

    parts = [[chunk] for chunk in plan.chunks]
    fields = []
    for p, chunks in enumerate(parts):
        field = shape(len(chunks), plan.rows, plan.tiles, SUBS, LANES)
        edge = shape(len(chunks), halo, plan.tiles, SUBS, LANES)
        field, inner, outer = call(
            functools.partial(arrange_kernel, plan, chunks, p == 0),
            (field, edge, edge),
            increment[: chunks[0][1]] if p == 0 else increment,
            flops=10**7,
        )
        outer = lax.ppermute(outer, "tile", swap(1))
        inner = lax.ppermute(inner, "tile", swap(0))
        fields += [(c, field, inner, outer) for c in range(len(chunks))]

    def exchange(blocks):
        if not isinstance(blocks, tuple):
            return [lax.all_to_all(blocks, "lev", 0, 0, tiled=True)]
        got = {0: blocks[0]}
        for d in reversed(range(1, group)):
            got[d] = lax.ppermute(blocks[d], "lev", [(i, i ^ d) for i in range(group)])
        return [got[d] for d in range(group)]

    together = [c in TOGETHER_CHUNKS for c in range(len(plan.chunks))]
    held, counts = [], []
    for c, (first, count) in enumerate(plan.chunks):
        factor = jnp.pad(
            kappa[first : first + count], (0, SUBS - count), constant_values=0.125
        )
        factor = jnp.broadcast_to(factor[:, None], (SUBS, LANES))
        if count == SUBS:
            block = (plan.units, SUBS, LANES)
        else:
            block = (up_to(plan.units * count, SUBS), LANES)
        height = plan.rows_held + 2 * halo
        blocks = call(
            functools.partial(diffuse_kernel, plan, count, fields[c][0], together[c]),
            shape(group, *block) if together[c] else (shape(*block),) * group,
            *fields[c][1:],
            factor,
            scratch=[pltpu.VMEM((height, plan.tiles, SUBS, LANES), f32)] * 2,
            flops=10**9,
        )
        got = exchange(blocks)
        counts.append(len(got))
        held += got

    stride = up_to(levels, SUBS)
    operator = jax.ShapeDtypeStruct((group * stride, group * levels), jnp.bfloat16)
    high, low = call(
        functools.partial(operator_kernel, plan, together),
        (operator, operator),
        correlation,
        balance,
        flops=10**8,
    )

    half = plan.units // 2
    splits = [(0, half), (half, plan.units)]
    back = []
    for begin, stop in splits:
        block = shape(up_to((stop - begin) * levels, SUBS), LANES)
        blocks = call(
            functools.partial(mix_kernel, plan, counts, begin, stop),
            (block,) * group,
            high,
            low,
            *held,
            flops=10**9,
        )
        back.append(exchange(blocks))

    partly = call(
        functools.partial(unpack_kernel, plan, *splits[0]),
        shape(plan.tiles, levels * plan.rows_held, LANES),
        *back[0],
        flops=10**7,
    )
    return call(
        functools.partial(finish_kernel, plan, *splits[1]),
        shape(*increment.shape),
        ground_level,
        partly,
        *back[1],
        flops=10**7,
    )


def solution(mesh):
    return jax.shard_map(
        program,
        mesh=mesh,
        in_specs=(P("lev", "tile", None), P("lev"), P(), P(), P("tile", None)),
        out_specs=P("lev", "tile", None),
        check_vma=False,
    )
```

```python
import functools

import jax
import jax.numpy as jnp
from jax import lax
from jax.experimental import pallas as pl
from jax.experimental.pallas import tpu as pltpu
from jax.sharding import PartitionSpec as P


PASSES = 10
LANES = 128
SUBS = 8
UNROLLS = (4, 2)
DEAL = 4

VMEM = pl.BlockSpec(memory_space=pltpu.VMEM)
ANY = pl.BlockSpec(memory_space=pl.ANY)


def level_chunks(levels):
    chunks = [(first, SUBS) for first in range(0, levels - levels % SUBS, SUBS)]
    if levels % SUBS:
        chunks.append((levels - levels % SUBS, levels % SUBS))
    return chunks


def up_to(value, multiple):
    return -(-value // multiple) * multiple


class Plan:
    def __init__(self, shape, group):
        self.levels, self.rows, self.lons = shape
        self.group = group
        self.halo = PASSES
        self.full = self.lons // LANES
        self.rest = self.lons % LANES
        self.tiles = self.full + 1
        assert self.halo <= self.rest and self.rest + 2 * self.halo <= LANES
        assert PASSES % 2 == 0 and self.tiles % DEAL == 0 and self.rows % 2 == 0
        assert self.halo <= self.rows and group & (group - 1) == 0
        self.rows_each = -(-self.rows // group)
        self.rows_held = self.rows_each * group
        self.per_merged = LANES // self.rest
        self.merged = -(-self.rows_each // self.per_merged)
        self.units = self.rows_each * self.full + self.merged
        self.chunks = level_chunks(self.levels)


def lane_ids():
    return lax.broadcasted_iota(jnp.int32, (SUBS, LANES), 1)


def swapped(tiles):
    lane = lane_ids()
    even, low = (lane & 32) == 0, lane < 64
    a, b, c, d = tiles
    first, second = (
        (jnp.where(even, x, pltpu.roll(y, 32, 1)), jnp.where(even, pltpu.roll(x, 96, 1), y))
        for x, y in ((a, b), (c, d))
    )
    (a, b), (c, d) = first, second
    return [
        jnp.where(low, a, pltpu.roll(c, 64, 1)),
        jnp.where(low, b, pltpu.roll(d, 64, 1)),
        jnp.where(low, pltpu.roll(a, 64, 1), c),
        jnp.where(low, pltpu.roll(b, 64, 1), d),
    ]


def lanes_taken(value, index):
    return jnp.take_along_axis(value, index, axis=1, mode="promise_in_bounds")


def dealt(tiles):
    lane = lane_ids()
    index = 4 * (lane & 31) + (lane >> 5)
    return swapped([lanes_taken(tile, index) for tile in tiles])


def gathered(tiles):
    lane = lane_ids()
    index = 32 * (lane & 3) + (lane >> 2)
    return [lanes_taken(tile, index) for tile in swapped(tiles)]


def arrange_kernel(plan, chunks, alone, x_ref, all_ref, inner_ref, outer_ref):
    begin = chunks[0][0] if alone else 0
    lane = lane_ids()
    even = lax.axis_index("tile") % 2 == 0
    inner_row = jnp.where(even, plan.rows - plan.halo, 0)
    outer_row = jnp.where(even, 0, plan.rows - plan.halo)
    for c, (first, count) in enumerate(chunks):
        for row in range(plan.rows):

            def take(tile):
                width = LANES if tile < plan.full else plan.rest
                lanes = slice(tile * LANES, tile * LANES + width)
                value = x_ref[first - begin : first - begin + count, row, lanes]
                if count < SUBS or width < LANES:
                    value = jnp.pad(value, ((0, SUBS - count), (0, LANES - width)))
                return value

            values = [take(tile) for tile in range(plan.tiles)]
            last = values[-1]
            values[-1] = jnp.where(
                lane < plan.rest,
                last,
                jnp.where(
                    lane < plan.rest + plan.halo,
                    pltpu.roll(values[0], plan.rest, 1),
                    pltpu.roll(last, LANES - plan.rest, 1),
                ),
            )
            for tile, value in enumerate(values):
                all_ref[c, row, tile] = value

        unroll = next(u for u in UNROLLS if plan.rows % u == 0)

        def deal(step, _):
            for i in range(unroll):
                row = step * unroll + i
                for tile in range(0, plan.tiles, DEAL):
                    values = [all_ref[c, row, tile + b] for b in range(DEAL)]
                    for b, value in enumerate(dealt(values)):
                        all_ref[c, row, tile + b] = value
            return 0

        lax.fori_loop(0, plan.rows // unroll, deal, 0)
        for row in range(plan.halo):
            for tile in range(plan.tiles):
                inner_ref[c, row, tile] = all_ref[c, inner_row + row, tile]
                outer_ref[c, row, tile] = all_ref[c, outer_row + row, tile]


def diffuse(plan, at, chunk, kappa_ref, x_ref, inner_ref, outer_ref, a_ref, b_ref):
    tile_index = lax.axis_index("tile")
    height = plan.rows + 2 * plan.halo
    lane = lane_ids()
    at_start, at_end = lane == 0, lane == LANES - 1
    level = lax.broadcasted_iota(jnp.int32, (SUBS, LANES), 0)
    kappa = jnp.full((SUBS, LANES), 0.125, jnp.float32)
    for i in range(chunk[1]):
        kappa = jnp.where(level == i, kappa_ref[chunk[0] + i], kappa)
    ratio = (1.0 - 4.0 * kappa) / kappa
    kept = {
        plan.halo - 1: jnp.where(tile_index == 0, 0.0, 1.0),
        plan.halo + plan.rows: jnp.where(tile_index == lax.axis_size("tile") - 1, 0.0, 1.0),
    }
    below = plan.halo + plan.rows
    inner_row = jnp.where(tile_index % 2 == 0, below, 0)
    for row in range(plan.halo):
        a_ref[inner_row + row] = inner_ref[at, row]
        a_ref[below - inner_row + row] = outer_ref[at, row]
    a_ref[plan.halo : below] = x_ref[at]

    groups = range(0, plan.tiles, DEAL)

    def sweep(source, target, first, stop):
        def turned(row):
            left = [pltpu.roll(source[row, t], LANES - 1, 1) for t in groups]
            right = [pltpu.roll(source[row, t + DEAL - 1], 1, 1) for t in groups]
            return left, right

        ahead = turned(first)
        for row in range(first, stop):
            left, right = ahead
            if row + 1 < stop:
                ahead = turned(row + 1)
            here = [source[row, tile] for tile in range(plan.tiles)]
            for tile in range(plan.tiles):
                g = tile // DEAL
                if tile % DEAL == 0:
                    west = jnp.where(at_start, right[g - 1], right[g])
                else:
                    west = here[tile - 1]
                if tile % DEAL == DEAL - 1:
                    east = jnp.where(at_end, left[(g + 1) % len(groups)], left[g])
                else:
                    east = here[tile + 1]
                beside = (source[row - 1, tile] + source[row + 1, tile]) + (west + east)
                value = ratio * here[tile] + beside
                target[row, tile] = value * kept[row] if row in kept else value

    def two_passes(done):
        def body(step, _):
            sweep(a_ref, b_ref, done + 1, height - 1 - done)
            sweep(b_ref, a_ref, done + 2, height - 2 - done)
            return 0

        return body

    early = PASSES // 4
    lax.fori_loop(0, early, two_passes(0), 0)
    lax.fori_loop(early, PASSES // 2, two_passes(2 * early), 0)
    power = kappa
    for _ in range(PASSES - 1):
        power = power * kappa

    unroll = next(u for u in UNROLLS if plan.rows % u == 0)

    def undo(step, _):
        for i in range(unroll):
            row = step * unroll + i
            for tile in groups:
                values = [a_ref[plan.halo + row, tile + b] * power for b in range(DEAL)]
                for b, value in enumerate(gathered(values)):
                    b_ref[row, tile + b] = value
        return 0

    lax.fori_loop(0, plan.rows // unroll, undo, 0)


def block_rows(parts, units):
    first = [0]
    for count in parts:
        first.append(first[-1] + up_to(units * count, SUBS))
    return first


def diffuse_kernel(plan, chunks, splits, *refs):
    parts = [count for _, count in chunks]
    given, out_refs, (a_ref, b_ref) = refs[:4], refs[4:-2], refs[-2:]
    me = lax.axis_index("lev")
    lane = lane_ids()
    for p, count in enumerate(parts):
        diffuse(plan, p, chunks[p], *given, a_ref, b_ref)
        for d in range(plan.group):
            base = (me ^ d) * plan.rows_each

            def put(unit, value):
                for s, (begin, stop) in enumerate(splits):
                    if begin <= unit < stop:
                        row = block_rows(parts, stop - begin)[p] + (unit - begin) * count
                        out_refs[s * plan.group + d][row : row + count] = value[:count]

            for i in range(plan.rows_each):
                for tile in range(plan.full):
                    put(i * plan.full + tile, b_ref[base + i, tile])
            for m in range(plan.merged):
                value = None
                for k in range(plan.per_merged):
                    i = m * plan.per_merged + k
                    if i < plan.rows_each:
                        piece = b_ref[base + i, plan.full]
                        if k == 0:
                            value = piece
                        else:
                            value = jnp.where(
                                lane < k * plan.rest, value, pltpu.roll(piece, k * plan.rest, 1)
                            )
                put(plan.rows_each * plan.full + m, value)


def operator_kernel(plan, correlation_ref, balance_ref, high_ref, low_ref):
    group, levels = plan.group, plan.levels
    stride = up_to(levels, SUBS)
    me = lax.axis_index("lev")

    def exact(left, right, dims=((1,), (0,))):
        return lax.dot_general(
            left,
            right,
            (dims, ((), ())),
            precision=lax.Precision.HIGHEST,
            preferred_element_type=jnp.float32,
        )

    def picked(shape, pieces):
        place = lax.broadcasted_iota(jnp.int32, shape, 0)
        level = jnp.full(shape, -1, jnp.int32)
        for first, count, start in pieces:
            here = (place >= first) & (place < first + count)
            level = jnp.where(here, start + place - first, level)
        return (level == lax.broadcasted_iota(jnp.int32, shape, 1)).astype(jnp.float32)

    rows = [(d * stride, levels, (me ^ d) * levels) for d in range(group)]
    columns, place = [], 0
    for first, count in plan.chunks:
        for d in range(group):
            columns.append((place, count, (me ^ d) * levels + first))
            place += count
    left = exact(picked((group * stride, group * levels), rows), correlation_ref[...])
    right = exact(
        balance_ref[...], picked((group * levels, group * levels), columns), ((1,), (1,))
    )
    operator = exact(left, right)
    high = operator.astype(jnp.bfloat16)
    high_ref[...] = high
    low_ref[...] = (operator - high.astype(jnp.float32)).astype(jnp.bfloat16)


def mix_kernel(plan, sources, first, stop, high_ref, low_ref, *refs):
    group, levels = plan.group, plan.levels
    out_refs = refs[len(sources) * group :]
    high, low = high_ref[...], low_ref[...]
    stride = up_to(levels, SUBS)
    for unit in range(first, stop):
        pieces = []
        for g, (parts, begin, end) in enumerate(sources):
            starts = block_rows(parts, end - begin)
            for p, count in enumerate(parts):
                row = starts[p] + (unit - begin) * count
                pieces += [block[row : row + count] for block in refs[g * group : (g + 1) * group]]
        column = jnp.concatenate(pieces, axis=0)
        column_high = column.astype(jnp.bfloat16)
        column_low = (column - column_high.astype(jnp.float32)).astype(jnp.bfloat16)

        def dot(matrix, values):
            return jnp.dot(matrix, values, preferred_element_type=jnp.float32)

        result = dot(high, column_high) + (dot(high, column_low) + dot(low, column_high))
        for d in range(group):
            out_refs[d][(unit - first) * levels : (unit - first + 1) * levels] = result[
                d * stride : d * stride + levels
            ]


def unpack(plan, begin, stop, received, held_ref):
    levels, rows_held = plan.levels, plan.rows_held
    me = lax.axis_index("lev")

    def store(tile, row, value):
        for first in range(0, levels, SUBS):
            count = min(SUBS, levels - first)
            held_ref[tile, pl.ds(row + first * rows_held, count, stride=rows_held), :] = value[
                first : first + count
            ]

    for d in range(plan.group):
        base = (me ^ d) * plan.rows_each
        for unit in range(begin, stop):
            value = received[d][(unit - begin) * levels : (unit - begin + 1) * levels]
            if unit < plan.rows_each * plan.full:
                store(unit % plan.full, base + unit // plan.full, value)
            else:
                m = unit - plan.rows_each * plan.full
                for k in range(plan.per_merged):
                    i = m * plan.per_merged + k
                    if i < plan.rows_each:
                        piece = pltpu.roll(value, LANES - k * plan.rest, 1) if k else value
                        store(plan.full, base + i, piece)


def unpack_kernel(plan, begin, stop, *refs):
    unpack(plan, begin, stop, refs[:-1], refs[-1])


def finish_kernel(plan, begin, stop, ground_ref, held_ref, *refs):
    out_ref = refs[plan.group]
    levels, rows_held = plan.levels, plan.rows_held
    unpack(plan, begin, stop, refs[: plan.group], held_ref)
    me = lax.axis_index("lev")
    for tile in range(plan.tiles):
        width = LANES if tile < plan.full else plan.rest
        lanes = slice(tile * LANES, tile * LANES + width)
        ground = ground_ref[:, lanes]
        for level in range(levels):
            value = held_ref[tile, level * rows_held : level * rows_held + plan.rows, :width]
            out_ref[level, :, lanes] = jnp.where(me * levels + level < ground, value, 0.0)


def program(increment, kappa, balance, correlation, ground_level):
    group = lax.axis_size("lev")
    tiles_around = lax.axis_size("tile")
    plan = Plan(increment.shape, group)
    levels, halo = plan.levels, plan.halo
    f32 = jnp.float32

    def shape(*dims):
        return jax.ShapeDtypeStruct(dims, f32)

    def call(kernel, outs, *args, scratch=(), flops, first_spec=VMEM):
        return pl.pallas_call(
            kernel,
            out_shape=outs,
            in_specs=[first_spec] + [VMEM] * (len(args) - 1),
            out_specs=jax.tree.map(lambda _: VMEM, outs),
            scratch_shapes=list(scratch),
            compiler_params=pltpu.CompilerParams(vmem_limit_bytes=14 << 20),
            cost_estimate=pl.CostEstimate(flops=flops, bytes_accessed=1 << 20, transcendentals=0),
        )(*args)

    def swap(start):
        return [(i + k, i + 1 - k) for i in range(start, tiles_around - 1, 2) for k in range(2)]

    steps = [chunks for chunks in (plan.chunks[:1], plan.chunks[1:]) if chunks]
    fields = []
    for g, chunks in enumerate(steps):
        field = shape(len(chunks), plan.rows, plan.tiles, SUBS, LANES)
        edge = shape(len(chunks), halo, plan.tiles, SUBS, LANES)
        field, inner, outer = call(
            functools.partial(arrange_kernel, plan, chunks, g == 0),
            (field, edge, edge),
            increment[: chunks[0][1]] if g == 0 else increment,
            flops=10**7,
        )
        outer = lax.ppermute(outer, "tile", swap(1))
        inner = lax.ppermute(inner, "tile", swap(0))
        fields.append((field, inner, outer))

    def exchange(blocks):
        got = {0: blocks[0]}
        for d in range(1, group):
            got[d] = lax.ppermute(blocks[d], "lev", [(i, i ^ d) for i in range(group)])
        return [got[d] for d in range(group)]

    whole = [(0, plan.units)]
    half = plan.units // 2
    splits = [(0, half), (half, plan.units)]
    height = plan.rows_held + 2 * halo
    sources = [[] for _ in splits]
    held = [[] for _ in splits]
    for g, chunks in enumerate(steps):
        parts = [count for _, count in chunks]
        cuts = splits if g else whole
        outs = []
        for begin, stop in cuts:
            outs += [shape(block_rows(parts, stop - begin)[-1], LANES)] * group
        blocks = call(
            functools.partial(diffuse_kernel, plan, chunks, cuts),
            tuple(outs),
            kappa,
            *fields[g],
            scratch=[pltpu.VMEM((height, plan.tiles, SUBS, LANES), f32)] * 2,
            flops=10**9,
            first_spec=pl.BlockSpec(memory_space=pltpu.SMEM),
        )
        for s, (begin, stop) in enumerate(cuts):
            got = exchange(blocks[s * group : (s + 1) * group])
            for t in range(len(splits)):
                if len(cuts) == 1 or s == t:
                    sources[t].append((parts, begin, stop))
                    held[t] += got

    stride = up_to(levels, SUBS)
    operator = jax.ShapeDtypeStruct((group * stride, group * levels), jnp.bfloat16)
    high, low = call(
        functools.partial(operator_kernel, plan),
        (operator, operator),
        correlation,
        balance,
        flops=10**8,
    )

    back = []
    for s, (begin, stop) in enumerate(splits):
        block = shape(up_to((stop - begin) * levels, SUBS), LANES)
        blocks = call(
            functools.partial(mix_kernel, plan, sources[s], begin, stop),
            (block,) * group,
            high,
            low,
            *held[s],
            flops=10**9,
        )
        back.append(exchange(blocks))

    partly = call(
        functools.partial(unpack_kernel, plan, *splits[0]),
        shape(plan.tiles, levels * plan.rows_held, LANES),
        *back[0],
        flops=10**7,
    )
    return call(
        functools.partial(finish_kernel, plan, *splits[1]),
        shape(*increment.shape),
        ground_level,
        partly,
        *back[1],
        flops=10**7,
    )


def solution(mesh):
    return jax.shard_map(
        program,
        mesh=mesh,
        in_specs=(P("lev", "tile", None), P("lev"), P(), P(), P("tile", None)),
        out_specs=P("lev", "tile", None),
        check_vma=False,
    )
```

```python
import functools

import jax
import jax.numpy as jnp
from jax import lax
from jax.experimental import pallas as pl
from jax.experimental.pallas import tpu as pltpu
from jax.sharding import PartitionSpec as P


PASSES = 10
LANES = 128
SUBS = 8
UNROLLS = (4, 2)
DEAL = 4

VMEM = pl.BlockSpec(memory_space=pltpu.VMEM)
ANY = pl.BlockSpec(memory_space=pl.ANY)


def level_chunks(levels):
    chunks = [(first, SUBS) for first in range(0, levels - levels % SUBS, SUBS)]
    if levels % SUBS:
        chunks.append((levels - levels % SUBS, levels % SUBS))
    return chunks


def up_to(value, multiple):
    return -(-value // multiple) * multiple


class Plan:
    def __init__(self, shape, group):
        self.levels, self.rows, self.lons = shape
        self.group = group
        self.halo = PASSES
        self.full = self.lons // LANES
        self.rest = self.lons % LANES
        self.tiles = self.full + 1
        assert self.halo <= self.rest and self.rest + 2 * self.halo <= LANES
        assert PASSES % 2 == 0 and self.tiles % DEAL == 0 and self.rows % 2 == 0
        assert self.halo <= self.rows and group & (group - 1) == 0
        self.rows_each = -(-self.rows // group)
        self.rows_held = self.rows_each * group
        self.per_merged = LANES // self.rest
        self.merged = -(-self.rows_each // self.per_merged)
        self.units = self.rows_each * self.full + self.merged
        self.chunks = level_chunks(self.levels)


def lane_ids():
    return lax.broadcasted_iota(jnp.int32, (SUBS, LANES), 1)


def swapped(tiles):
    lane = lane_ids()
    even, low = (lane & 32) == 0, lane < 64
    a, b, c, d = tiles
    first, second = (
        (jnp.where(even, x, pltpu.roll(y, 32, 1)), jnp.where(even, pltpu.roll(x, 96, 1), y))
        for x, y in ((a, b), (c, d))
    )
    (a, b), (c, d) = first, second
    return [
        jnp.where(low, a, pltpu.roll(c, 64, 1)),
        jnp.where(low, b, pltpu.roll(d, 64, 1)),
        jnp.where(low, pltpu.roll(a, 64, 1), c),
        jnp.where(low, pltpu.roll(b, 64, 1), d),
    ]


def lanes_taken(value, index):
    return jnp.take_along_axis(value, index, axis=1, mode="promise_in_bounds")


def dealt(tiles):
    lane = lane_ids()
    index = 4 * (lane & 31) + (lane >> 5)
    return swapped([lanes_taken(tile, index) for tile in tiles])


def gathered(tiles):
    lane = lane_ids()
    index = 32 * (lane & 3) + (lane >> 2)
    return [lanes_taken(tile, index) for tile in swapped(tiles)]


def arrange_kernel(plan, chunks, alone, x_ref, all_ref, inner_ref, outer_ref):
    begin = chunks[0][0] if alone else 0
    lane = lane_ids()
    even = lax.axis_index("tile") % 2 == 0
    inner_row = jnp.where(even, plan.rows - plan.halo, 0)
    outer_row = jnp.where(even, 0, plan.rows - plan.halo)
    for c, (first, count) in enumerate(chunks):
        for row in range(plan.rows):

            def take(tile):
                width = LANES if tile < plan.full else plan.rest
                lanes = slice(tile * LANES, tile * LANES + width)
                value = x_ref[first - begin : first - begin + count, row, lanes]
                if count < SUBS or width < LANES:
                    value = jnp.pad(value, ((0, SUBS - count), (0, LANES - width)))
                return value

            values = [take(tile) for tile in range(plan.tiles)]
            last = values[-1]
            values[-1] = jnp.where(
                lane < plan.rest,
                last,
                jnp.where(
                    lane < plan.rest + plan.halo,
                    pltpu.roll(values[0], plan.rest, 1),
                    pltpu.roll(last, LANES - plan.rest, 1),
                ),
            )
            for tile, value in enumerate(values):
                all_ref[c, row, tile] = value

        unroll = next(u for u in UNROLLS if plan.rows % u == 0)

        def deal(step, _):
            for i in range(unroll):
                row = step * unroll + i
                for tile in range(0, plan.tiles, DEAL):
                    values = [all_ref[c, row, tile + b] for b in range(DEAL)]
                    for b, value in enumerate(dealt(values)):
                        all_ref[c, row, tile + b] = value
            return 0

        lax.fori_loop(0, plan.rows // unroll, deal, 0)
        for row in range(plan.halo):
            for tile in range(plan.tiles):
                inner_ref[c, row, tile] = all_ref[c, inner_row + row, tile]
                outer_ref[c, row, tile] = all_ref[c, outer_row + row, tile]


def diffuse(plan, at, chunk, kappa_ref, x_ref, inner_ref, outer_ref, a_ref, b_ref):
    tile_index = lax.axis_index("tile")
    height = plan.rows + 2 * plan.halo
    lane = lane_ids()
    at_start, at_end = lane == 0, lane == LANES - 1
    level = lax.broadcasted_iota(jnp.int32, (SUBS, LANES), 0)
    kappa = jnp.full((SUBS, LANES), 0.125, jnp.float32)
    for i in range(chunk[1]):
        kappa = jnp.where(level == i, kappa_ref[chunk[0] + i], kappa)
    ratio = (1.0 - 4.0 * kappa) / kappa
    kept = {
        plan.halo - 1: jnp.where(tile_index == 0, 0.0, 1.0),
        plan.halo + plan.rows: jnp.where(tile_index == lax.axis_size("tile") - 1, 0.0, 1.0),
    }
    below = plan.halo + plan.rows
    inner_row = jnp.where(tile_index % 2 == 0, below, 0)
    for row in range(plan.halo):
        a_ref[inner_row + row] = inner_ref[at, row]
        a_ref[below - inner_row + row] = outer_ref[at, row]
    a_ref[plan.halo : below] = x_ref[at]

    groups = range(0, plan.tiles, DEAL)

    def sweep(source, target, first, stop):
        def turned(row):
            left = [pltpu.roll(source[row, t], LANES - 1, 1) for t in groups]
            right = [pltpu.roll(source[row, t + DEAL - 1], 1, 1) for t in groups]
            return left, right

        ahead = turned(first)
        for row in range(first, stop):
            left, right = ahead
            if row + 1 < stop:
                ahead = turned(row + 1)
            here = [source[row, tile] for tile in range(plan.tiles)]
            for tile in range(plan.tiles):
                g = tile // DEAL
                if tile % DEAL == 0:
                    west = jnp.where(at_start, right[g - 1], right[g])
                else:
                    west = here[tile - 1]
                if tile % DEAL == DEAL - 1:
                    east = jnp.where(at_end, left[(g + 1) % len(groups)], left[g])
                else:
                    east = here[tile + 1]
                beside = (source[row - 1, tile] + source[row + 1, tile]) + (west + east)
                value = ratio * here[tile] + beside
                target[row, tile] = value * kept[row] if row in kept else value

    def two_passes(done):
        def body(step, _):
            sweep(a_ref, b_ref, done + 1, height - 1 - done)
            sweep(b_ref, a_ref, done + 2, height - 2 - done)
            return 0

        return body

    early = PASSES // 4
    lax.fori_loop(0, early, two_passes(0), 0)
    lax.fori_loop(early, PASSES // 2, two_passes(2 * early), 0)
    power = kappa
    for _ in range(PASSES - 1):
        power = power * kappa

    unroll = next(u for u in UNROLLS if plan.rows % u == 0)

    def undo(step, _):
        for i in range(unroll):
            row = step * unroll + i
            for tile in groups:
                values = [a_ref[plan.halo + row, tile + b] * power for b in range(DEAL)]
                for b, value in enumerate(gathered(values)):
                    b_ref[row, tile + b] = value
        return 0

    lax.fori_loop(0, plan.rows // unroll, undo, 0)


def block_rows(parts, units):
    first = [0]
    for count in parts:
        first.append(first[-1] + up_to(units * count, SUBS))
    return first


def diffuse_kernel(plan, chunks, splits, *refs):
    parts = [count for _, count in chunks]
    given, out_refs, (a_ref, b_ref) = refs[:4], refs[4:-2], refs[-2:]
    me = lax.axis_index("lev")
    lane = lane_ids()
    for p, count in enumerate(parts):
        diffuse(plan, p, chunks[p], *given, a_ref, b_ref)
        for d in range(plan.group):
            base = (me ^ d) * plan.rows_each

            def put(unit, value):
                for s, (begin, stop) in enumerate(splits):
                    if begin <= unit < stop:
                        row = block_rows(parts, stop - begin)[p] + (unit - begin) * count
                        out_refs[s * plan.group + d][row : row + count] = value[:count]

            for i in range(plan.rows_each):
                for tile in range(plan.full):
                    put(tile * plan.rows_each + i, b_ref[base + i, tile])
            for m in range(plan.merged):
                value = None
                for k in range(plan.per_merged):
                    i = m * plan.per_merged + k
                    if i < plan.rows_each:
                        piece = b_ref[base + i, plan.full]
                        if k == 0:
                            value = piece
                        else:
                            value = jnp.where(
                                lane < k * plan.rest, value, pltpu.roll(piece, k * plan.rest, 1)
                            )
                put(plan.rows_each * plan.full + m, value)


def operator_kernel(plan, correlation_ref, balance_ref, high_ref, low_ref):
    group, levels = plan.group, plan.levels
    stride = up_to(levels, SUBS)
    me = lax.axis_index("lev")

    def exact(left, right, dims=((1,), (0,))):
        return lax.dot_general(
            left,
            right,
            (dims, ((), ())),
            precision=lax.Precision.HIGHEST,
            preferred_element_type=jnp.float32,
        )

    def picked(shape, pieces):
        place = lax.broadcasted_iota(jnp.int32, shape, 0)
        level = jnp.full(shape, -1, jnp.int32)
        for first, count, start in pieces:
            here = (place >= first) & (place < first + count)
            level = jnp.where(here, start + place - first, level)
        return (level == lax.broadcasted_iota(jnp.int32, shape, 1)).astype(jnp.float32)

    rows = [(d * stride, levels, (me ^ d) * levels) for d in range(group)]
    columns, place = [], 0
    for first, count in plan.chunks:
        for d in range(group):
            columns.append((place, count, (me ^ d) * levels + first))
            place += count
    left = exact(picked((group * stride, group * levels), rows), correlation_ref[...])
    right = exact(
        balance_ref[...], picked((group * levels, group * levels), columns), ((1,), (1,))
    )
    operator = exact(left, right)
    high = operator.astype(jnp.bfloat16)
    high_ref[...] = high
    low_ref[...] = (operator - high.astype(jnp.float32)).astype(jnp.bfloat16)


def mix_kernel(plan, sources, first, stop, high_ref, low_ref, *refs):
    group, levels = plan.group, plan.levels
    out_refs = refs[len(sources) * group :]
    high, low = high_ref[...], low_ref[...]
    stride = up_to(levels, SUBS)
    for unit in range(first, stop):
        pieces = []
        for g, (parts, begin, end) in enumerate(sources):
            starts = block_rows(parts, end - begin)
            for p, count in enumerate(parts):
                row = starts[p] + (unit - begin) * count
                pieces += [block[row : row + count] for block in refs[g * group : (g + 1) * group]]
        column = jnp.concatenate(pieces, axis=0)
        column_high = column.astype(jnp.bfloat16)
        column_low = (column - column_high.astype(jnp.float32)).astype(jnp.bfloat16)

        def dot(matrix, values):
            return jnp.dot(matrix, values, preferred_element_type=jnp.float32)

        result = dot(high, column_high) + (dot(high, column_low) + dot(low, column_high))
        for d in range(group):
            out_refs[d][(unit - first) * levels : (unit - first + 1) * levels] = result[
                d * stride : d * stride + levels
            ]


def finish_kernel(plan, begin, stop, tiles, ground_ref, *refs):
    received, (out_ref, held_ref) = refs[: plan.group], refs[-2:]
    levels, rows_held = plan.levels, plan.rows_held
    me = lax.axis_index("lev")

    def store(tile, row, value):
        for first in range(0, levels, SUBS):
            count = min(SUBS, levels - first)
            held_ref[tile - tiles[0], pl.ds(row + first * rows_held, count, stride=rows_held), :] = (
                value[first : first + count]
            )

    for d in range(plan.group):
        base = (me ^ d) * plan.rows_each
        for unit in range(begin, stop):
            value = received[d][(unit - begin) * levels : (unit - begin + 1) * levels]
            if unit < plan.rows_each * plan.full:
                store(unit // plan.rows_each, base + unit % plan.rows_each, value)
            else:
                m = unit - plan.rows_each * plan.full
                for k in range(plan.per_merged):
                    i = m * plan.per_merged + k
                    if i < plan.rows_each:
                        piece = pltpu.roll(value, LANES - k * plan.rest, 1) if k else value
                        store(plan.full, base + i, piece)
    for tile in tiles:
        width = LANES if tile < plan.full else plan.rest
        lanes = slice(tile * LANES, tile * LANES + width)
        here = slice((tile - tiles[0]) * LANES, (tile - tiles[0]) * LANES + width)
        ground = ground_ref[:, lanes]
        for level in range(levels):
            value = held_ref[
                tile - tiles[0], level * rows_held : level * rows_held + plan.rows, :width
            ]
            out_ref[level, :, here] = jnp.where(me * levels + level < ground, value, 0.0)


def program(increment, kappa, balance, correlation, ground_level):
    group = lax.axis_size("lev")
    tiles_around = lax.axis_size("tile")
    plan = Plan(increment.shape, group)
    levels, halo = plan.levels, plan.halo
    f32 = jnp.float32

    def shape(*dims):
        return jax.ShapeDtypeStruct(dims, f32)

    def call(kernel, outs, *args, scratch=(), flops, first_spec=VMEM):
        return pl.pallas_call(
            kernel,
            out_shape=outs,
            in_specs=[first_spec] + [VMEM] * (len(args) - 1),
            out_specs=jax.tree.map(lambda _: VMEM, outs),
            scratch_shapes=list(scratch),
            compiler_params=pltpu.CompilerParams(vmem_limit_bytes=14 << 20),
            cost_estimate=pl.CostEstimate(flops=flops, bytes_accessed=1 << 20, transcendentals=0),
        )(*args)

    def swap(start):
        return [(i + k, i + 1 - k) for i in range(start, tiles_around - 1, 2) for k in range(2)]

    steps = [chunks for chunks in (plan.chunks[:1], plan.chunks[1:]) if chunks]
    fields = []
    for g, chunks in enumerate(steps):
        field = shape(len(chunks), plan.rows, plan.tiles, SUBS, LANES)
        edge = shape(len(chunks), halo, plan.tiles, SUBS, LANES)
        field, inner, outer = call(
            functools.partial(arrange_kernel, plan, chunks, g == 0),
            (field, edge, edge),
            increment[: chunks[0][1]] if g == 0 else increment,
            flops=10**7,
        )
        inner = lax.ppermute(inner, "tile", swap(0))
        outer = lax.ppermute(outer, "tile", swap(1))
        fields.append((field, inner, outer))

    def exchange(blocks):
        got = {0: blocks[0]}
        for d in range(1, group):
            got[d] = lax.ppermute(blocks[d], "lev", [(i, i ^ d) for i in range(group)])
        return [got[d] for d in range(group)]

    whole = [(0, plan.units)]
    cut = (plan.full + 1) // 2
    half = cut * plan.rows_each
    splits = [(0, half), (half, plan.units)]
    height = plan.rows_held + 2 * halo
    sources = [[] for _ in splits]
    held = [[] for _ in splits]
    for g, chunks in enumerate(steps):
        parts = [count for _, count in chunks]
        cuts = splits if g else whole
        outs = []
        for begin, stop in cuts:
            outs += [shape(block_rows(parts, stop - begin)[-1], LANES)] * group
        blocks = call(
            functools.partial(diffuse_kernel, plan, chunks, cuts),
            tuple(outs),
            kappa,
            *fields[g],
            scratch=[pltpu.VMEM((height, plan.tiles, SUBS, LANES), f32)] * 2,
            flops=10**9,
            first_spec=pl.BlockSpec(memory_space=pltpu.SMEM),
        )
        for s, (begin, stop) in enumerate(cuts):
            got = exchange(blocks[s * group : (s + 1) * group])
            for t in range(len(splits)):
                if len(cuts) == 1 or s == t:
                    sources[t].append((parts, begin, stop))
                    held[t] += got

    stride = up_to(levels, SUBS)
    operator = jax.ShapeDtypeStruct((group * stride, group * levels), jnp.bfloat16)
    high, low = call(
        functools.partial(operator_kernel, plan),
        (operator, operator),
        correlation,
        balance,
        flops=10**8,
    )

    back = []
    for s, (begin, stop) in enumerate(splits):
        block = shape(up_to((stop - begin) * levels, SUBS), LANES)
        blocks = call(
            functools.partial(mix_kernel, plan, sources[s], begin, stop),
            (block,) * group,
            high,
            low,
            *held[s],
            flops=10**9,
        )
        back.append(exchange(blocks))

    result = ()
    for s, tiles in enumerate((range(cut), range(cut, plan.tiles))):
        assert len(tiles) <= cut or s == 1 and len(tiles) == cut
        result = (
            pl.pallas_call(
                functools.partial(finish_kernel, plan, *splits[s], tiles),
                grid=(1,),
                out_shape=shape(*increment.shape),
                in_specs=[VMEM] * (group + 1) + [pl.BlockSpec(memory_space=pl.ANY)] * s,
                out_specs=pl.BlockSpec((levels, plan.rows, cut * LANES), lambda _, s=s: (0, 0, s)),
                scratch_shapes=[pltpu.VMEM((cut, levels * plan.rows_held, LANES), f32)],
                input_output_aliases={group + 1: 0} if s else {},
                compiler_params=pltpu.CompilerParams(vmem_limit_bytes=14 << 20),
                cost_estimate=pl.CostEstimate(
                    flops=10**7, bytes_accessed=1 << 20, transcendentals=0
                ),
            )(ground_level, *back[s], *result),
        )
    return result[0]


def solution(mesh):
    return jax.shard_map(
        program,
        mesh=mesh,
        in_specs=(P("lev", "tile", None), P("lev"), P(), P(), P("tile", None)),
        out_specs=P("lev", "tile", None),
        check_vma=False,
    )
```

```python
import functools

import jax
import jax.numpy as jnp
from jax import lax
from jax.experimental import pallas as pl
from jax.experimental.pallas import tpu as pltpu
from jax.sharding import PartitionSpec as P


PASSES = 10
LANES = 128
SUBS = 8
UNROLLS = (6, 4, 2)
DEAL = 4

VMEM = pl.BlockSpec(memory_space=pltpu.VMEM)
ANY = pl.BlockSpec(memory_space=pl.ANY)


def level_chunks(levels):
    chunks = [(first, SUBS) for first in range(0, levels - levels % SUBS, SUBS)]
    if levels % SUBS:
        chunks.append((levels - levels % SUBS, levels % SUBS))
    return chunks


def up_to(value, multiple):
    return -(-value // multiple) * multiple


class Plan:
    def __init__(self, shape, group):
        self.levels, self.rows, self.lons = shape
        self.group = group
        self.halo = PASSES
        self.full = self.lons // LANES
        self.rest = self.lons % LANES
        self.tiles = self.full + 1
        assert self.halo <= self.rest and self.rest + 2 * self.halo <= LANES
        assert PASSES % 2 == 0 and self.tiles % DEAL == 0 and self.rows % 2 == 0
        assert self.halo <= self.rows and group & (group - 1) == 0
        self.rows_each = -(-self.rows // group)
        self.rows_held = self.rows_each * group
        self.per_merged = LANES // self.rest
        self.merged = -(-self.rows_each // self.per_merged)
        self.units = self.rows_each * self.full + self.merged
        self.chunks = level_chunks(self.levels)

    def edge_places(self, chunks):
        places, used = [], 0
        for c, (_, count) in enumerate(chunks):
            share = SUBS // count
            for row in range(self.halo):
                places.append((c, row, used + row // share, row % share * count))
            used += -(-self.halo // share)
        return places, used


def lane_ids():
    return lax.broadcasted_iota(jnp.int32, (SUBS, LANES), 1)


def swapped(tiles):
    lane = lane_ids()
    even, low = (lane & 32) == 0, lane < 64
    a, b, c, d = tiles
    first, second = (
        (jnp.where(even, x, pltpu.roll(y, 32, 1)), jnp.where(even, pltpu.roll(x, 96, 1), y))
        for x, y in ((a, b), (c, d))
    )
    (a, b), (c, d) = first, second
    return [
        jnp.where(low, a, pltpu.roll(c, 64, 1)),
        jnp.where(low, b, pltpu.roll(d, 64, 1)),
        jnp.where(low, pltpu.roll(a, 64, 1), c),
        jnp.where(low, pltpu.roll(b, 64, 1), d),
    ]


def lanes_taken(value, index):
    return jnp.take_along_axis(value, index, axis=1, mode="promise_in_bounds")


def dealt(tiles):
    lane = lane_ids()
    index = 4 * (lane & 31) + (lane >> 5)
    return swapped([lanes_taken(tile, index) for tile in tiles])


def gathered(tiles):
    lane = lane_ids()
    index = 32 * (lane & 3) + (lane >> 2)
    return [lanes_taken(tile, index) for tile in swapped(tiles)]


def arrange_kernel(plan, chunks, alone, x_ref, all_ref, inner_ref, outer_ref):
    begin = chunks[0][0] if alone else 0
    lane = lane_ids()
    even = lax.axis_index("tile") % 2 == 0
    inner_row = jnp.where(even, plan.rows - plan.halo, 0)
    outer_row = jnp.where(even, 0, plan.rows - plan.halo)
    for c, (first, count) in enumerate(chunks):
        for row in range(plan.rows):

            def take(tile):
                width = LANES if tile < plan.full else plan.rest
                lanes = slice(tile * LANES, tile * LANES + width)
                value = x_ref[first - begin : first - begin + count, row, lanes]
                if count < SUBS or width < LANES:
                    value = jnp.pad(value, ((0, SUBS - count), (0, LANES - width)))
                return value

            values = [take(tile) for tile in range(plan.tiles)]
            last = values[-1]
            values[-1] = jnp.where(
                lane < plan.rest,
                last,
                jnp.where(
                    lane < plan.rest + plan.halo,
                    pltpu.roll(values[0], plan.rest, 1),
                    pltpu.roll(last, LANES - plan.rest, 1),
                ),
            )
            for tile, value in enumerate(values):
                all_ref[c, row, tile] = value

        unroll = next(u for u in UNROLLS if plan.rows % u == 0)

        def deal(step, _):
            for i in range(unroll):
                row = step * unroll + i
                for tile in range(0, plan.tiles, DEAL):
                    values = [all_ref[c, row, tile + b] for b in range(DEAL)]
                    for b, value in enumerate(dealt(values)):
                        all_ref[c, row, tile + b] = value
            return 0

        lax.fori_loop(0, plan.rows // unroll, deal, 0)
    for c, row, place, sublane in plan.edge_places(chunks)[0]:
        count = chunks[c][1]
        here = slice(sublane, sublane + count)
        for tile in range(plan.tiles):
            inner_ref[place, tile, here] = all_ref[c, inner_row + row, tile, :count]
            outer_ref[place, tile, here] = all_ref[c, outer_row + row, tile, :count]


def diffuse(plan, at, chunks, kappa_ref, x_ref, inner_ref, outer_ref, a_ref, b_ref):
    tile_index = lax.axis_index("tile")
    height = plan.rows + 2 * plan.halo
    lane = lane_ids()
    at_start, at_end = lane == 0, lane == LANES - 1
    chunk = chunks[at]
    level = lax.broadcasted_iota(jnp.int32, (SUBS, LANES), 0)
    kappa = jnp.full((SUBS, LANES), 0.125, jnp.float32)
    for i in range(chunk[1]):
        kappa = jnp.where(level == i, kappa_ref[chunk[0] + i], kappa)
    ratio = (1.0 - 4.0 * kappa) / kappa
    kept = {
        plan.halo - 1: jnp.where(tile_index == 0, 0.0, 1.0),
        plan.halo + plan.rows: jnp.where(tile_index == lax.axis_size("tile") - 1, 0.0, 1.0),
    }
    below = plan.halo + plan.rows
    inner_row = jnp.where(tile_index % 2 == 0, below, 0)
    for c, row, place, sublane in plan.edge_places(chunks)[0]:
        if c == at:
            count = chunk[1]
            here = slice(sublane, sublane + count)
            for tile in range(plan.tiles):
                a_ref[inner_row + row, tile, :count] = inner_ref[place, tile, here]
                a_ref[below - inner_row + row, tile, :count] = outer_ref[place, tile, here]
    a_ref[plan.halo : below] = x_ref[at]

    groups = range(0, plan.tiles, DEAL)

    def sweep(source, target, first, stop):
        def turned(row):
            left = [pltpu.roll(source[row, t], LANES - 1, 1) for t in groups]
            right = [pltpu.roll(source[row, t + DEAL - 1], 1, 1) for t in groups]
            return left, right

        ahead = turned(first)
        for row in range(first, stop):
            left, right = ahead
            if row + 1 < stop:
                ahead = turned(row + 1)
            here = [source[row, tile] for tile in range(plan.tiles)]
            for tile in range(plan.tiles):
                g = tile // DEAL
                if tile % DEAL == 0:
                    west = jnp.where(at_start, right[g - 1], right[g])
                else:
                    west = here[tile - 1]
                if tile % DEAL == DEAL - 1:
                    east = jnp.where(at_end, left[(g + 1) % len(groups)], left[g])
                else:
                    east = here[tile + 1]
                beside = (source[row - 1, tile] + source[row + 1, tile]) + (west + east)
                value = ratio * here[tile] + beside
                target[row, tile] = value * kept[row] if row in kept else value

    def two_passes(done):
        def body(step, _):
            sweep(a_ref, b_ref, done + 1, height - 1 - done)
            sweep(b_ref, a_ref, done + 2, height - 2 - done)
            return 0

        return body

    early = PASSES // 4
    lax.fori_loop(0, early, two_passes(0), 0)
    lax.fori_loop(early, PASSES // 2, two_passes(2 * early), 0)
    power = kappa
    for _ in range(PASSES - 1):
        power = power * kappa

    unroll = next(u for u in UNROLLS if plan.rows % u == 0)

    def undo(step, _):
        for i in range(unroll):
            row = step * unroll + i
            for tile in groups:
                values = [a_ref[plan.halo + row, tile + b] * power for b in range(DEAL)]
                for b, value in enumerate(gathered(values)):
                    b_ref[row, tile + b] = value
        return 0

    lax.fori_loop(0, plan.rows // unroll, undo, 0)


def block_rows(parts, units):
    first = [0]
    for count in parts:
        first.append(first[-1] + up_to(units * count, SUBS))
    return first


def diffuse_kernel(plan, chunks, splits, *refs):
    parts = [count for _, count in chunks]
    given, out_refs, (a_ref, b_ref) = refs[:4], refs[4:-2], refs[-2:]
    me = lax.axis_index("lev")
    lane = lane_ids()
    for p, count in enumerate(parts):
        diffuse(plan, p, chunks, *given, a_ref, b_ref)
        for d in range(plan.group):
            base = (me ^ d) * plan.rows_each

            def put(unit, value):
                for s, (begin, stop) in enumerate(splits):
                    if begin <= unit < stop:
                        row = block_rows(parts, stop - begin)[p] + (unit - begin) * count
                        out_refs[s * plan.group + d][row : row + count] = value[:count]

            for i in range(plan.rows_each):
                for tile in range(plan.full):
                    put(tile * plan.rows_each + i, b_ref[base + i, tile])
            for m in range(plan.merged):
                value = None
                for k in range(plan.per_merged):
                    i = m * plan.per_merged + k
                    if i < plan.rows_each:
                        piece = b_ref[base + i, plan.full]
                        if k == 0:
                            value = piece
                        else:
                            value = jnp.where(
                                lane < k * plan.rest, value, pltpu.roll(piece, k * plan.rest, 1)
                            )
                put(plan.rows_each * plan.full + m, value)


def operator_kernel(plan, correlation_ref, balance_ref, high_ref, low_ref):
    group, levels = plan.group, plan.levels
    stride = up_to(levels, SUBS)
    me = lax.axis_index("lev")

    def exact(left, right, dims=((1,), (0,))):
        return lax.dot_general(
            left,
            right,
            (dims, ((), ())),
            precision=lax.Precision.HIGHEST,
            preferred_element_type=jnp.float32,
        )

    def picked(shape, pieces):
        place = lax.broadcasted_iota(jnp.int32, shape, 0)
        level = jnp.full(shape, -1, jnp.int32)
        for first, count, start in pieces:
            here = (place >= first) & (place < first + count)
            level = jnp.where(here, start + place - first, level)
        return (level == lax.broadcasted_iota(jnp.int32, shape, 1)).astype(jnp.float32)

    rows = [(d * stride, levels, (me ^ d) * levels) for d in range(group)]
    columns, place = [], 0
    for first, count in plan.chunks:
        for d in range(group):
            columns.append((place, count, (me ^ d) * levels + first))
            place += count
    left = exact(picked((group * stride, group * levels), rows), correlation_ref[...])
    right = exact(
        balance_ref[...], picked((group * levels, group * levels), columns), ((1,), (1,))
    )
    operator = exact(left, right)
    high = operator.astype(jnp.bfloat16)
    high_ref[...] = high
    low_ref[...] = (operator - high.astype(jnp.float32)).astype(jnp.bfloat16)


def mix_kernel(plan, sources, first, stop, high_ref, low_ref, *refs):
    group, levels = plan.group, plan.levels
    out_refs = refs[len(sources) * group :]
    high, low = high_ref[...], low_ref[...]
    stride = up_to(levels, SUBS)
    for unit in range(first, stop):
        pieces = []
        for g, (parts, begin, end) in enumerate(sources):
            starts = block_rows(parts, end - begin)
            for p, count in enumerate(parts):
                row = starts[p] + (unit - begin) * count
                pieces += [block[row : row + count] for block in refs[g * group : (g + 1) * group]]
        column = jnp.concatenate(pieces, axis=0)
        column_high = column.astype(jnp.bfloat16)
        column_low = (column - column_high.astype(jnp.float32)).astype(jnp.bfloat16)

        def dot(matrix, values):
            return jnp.dot(matrix, values, preferred_element_type=jnp.float32)

        result = dot(high, column_high) + (dot(high, column_low) + dot(low, column_high))
        for d in range(group):
            out_refs[d][(unit - first) * levels : (unit - first + 1) * levels] = result[
                d * stride : d * stride + levels
            ]


def finish_kernel(plan, begin, stop, tiles, ground_ref, *refs):
    received, (out_ref, held_ref) = refs[: plan.group], refs[-2:]
    levels, rows_held = plan.levels, plan.rows_held
    me = lax.axis_index("lev")

    def store(tile, row, value):
        for first in range(0, levels, SUBS):
            count = min(SUBS, levels - first)
            held_ref[tile - tiles[0], pl.ds(row + first * rows_held, count, stride=rows_held), :] = (
                value[first : first + count]
            )

    for d in range(plan.group):
        base = (me ^ d) * plan.rows_each
        for unit in range(begin, stop):
            value = received[d][(unit - begin) * levels : (unit - begin + 1) * levels]
            if unit < plan.rows_each * plan.full:
                store(unit // plan.rows_each, base + unit % plan.rows_each, value)
            else:
                m = unit - plan.rows_each * plan.full
                for k in range(plan.per_merged):
                    i = m * plan.per_merged + k
                    if i < plan.rows_each:
                        piece = pltpu.roll(value, LANES - k * plan.rest, 1) if k else value
                        store(plan.full, base + i, piece)
    for tile in tiles:
        width = LANES if tile < plan.full else plan.rest
        lanes = slice(tile * LANES, tile * LANES + width)
        here = slice((tile - tiles[0]) * LANES, (tile - tiles[0]) * LANES + width)
        ground = ground_ref[:, lanes]
        for level in range(levels):
            value = held_ref[
                tile - tiles[0], level * rows_held : level * rows_held + plan.rows, :width
            ]
            out_ref[level, :, here] = jnp.where(me * levels + level < ground, value, 0.0)


def program(increment, kappa, balance, correlation, ground_level):
    group = lax.axis_size("lev")
    tiles_around = lax.axis_size("tile")
    plan = Plan(increment.shape, group)
    levels, halo = plan.levels, plan.halo
    f32 = jnp.float32

    def shape(*dims):
        return jax.ShapeDtypeStruct(dims, f32)

    def call(kernel, outs, *args, scratch=(), flops, first_spec=VMEM):
        return pl.pallas_call(
            kernel,
            out_shape=outs,
            in_specs=[first_spec] + [VMEM] * (len(args) - 1),
            out_specs=jax.tree.map(lambda _: VMEM, outs),
            scratch_shapes=list(scratch),
            compiler_params=pltpu.CompilerParams(vmem_limit_bytes=14 << 20),
            cost_estimate=pl.CostEstimate(flops=flops, bytes_accessed=1 << 20, transcendentals=0),
        )(*args)

    def swap(start):
        return [(i + k, i + 1 - k) for i in range(start, tiles_around - 1, 2) for k in range(2)]

    steps = [chunks for chunks in (plan.chunks[:1], plan.chunks[1:]) if chunks]
    fields = []
    for g, chunks in enumerate(steps):
        field = shape(len(chunks), plan.rows, plan.tiles, SUBS, LANES)
        edge = shape(plan.edge_places(chunks)[1], plan.tiles, SUBS, LANES)
        field, inner, outer = call(
            functools.partial(arrange_kernel, plan, chunks, g == 0),
            (field, edge, edge),
            increment[: chunks[0][1]] if g == 0 else increment,
            flops=10**7,
        )
        inner = lax.ppermute(inner, "tile", swap(0))
        outer = lax.ppermute(outer, "tile", swap(1))
        fields.append((field, inner, outer))

    def exchange(blocks):
        got = {0: blocks[0]}
        for d in range(1, group):
            got[d] = lax.ppermute(blocks[d], "lev", [(i, i ^ d) for i in range(group)])
        return [got[d] for d in range(group)]

    whole = [(0, plan.units)]
    cut = 3 * plan.full // 4
    half = cut * plan.rows_each
    splits = [(0, half), (half, plan.units)]
    height = plan.rows_held + 2 * halo
    sources = [[] for _ in splits]
    held = [[] for _ in splits]
    for g, chunks in enumerate(steps):
        parts = [count for _, count in chunks]
        cuts = splits if g else whole
        outs = []
        for begin, stop in cuts:
            outs += [shape(block_rows(parts, stop - begin)[-1], LANES)] * group
        blocks = call(
            functools.partial(diffuse_kernel, plan, chunks, cuts),
            tuple(outs),
            kappa,
            *fields[g],
            scratch=[pltpu.VMEM((height, plan.tiles, SUBS, LANES), f32)] * 2,
            flops=10**9,
            first_spec=pl.BlockSpec(memory_space=pltpu.SMEM),
        )
        for s, (begin, stop) in enumerate(cuts):
            got = exchange(blocks[s * group : (s + 1) * group])
            for t in range(len(splits)):
                if len(cuts) == 1 or s == t:
                    sources[t].append((parts, begin, stop))
                    held[t] += got

    stride = up_to(levels, SUBS)
    operator = jax.ShapeDtypeStruct((group * stride, group * levels), jnp.bfloat16)
    high, low = call(
        functools.partial(operator_kernel, plan),
        (operator, operator),
        correlation,
        balance,
        flops=10**8,
    )

    back = []
    for s, (begin, stop) in enumerate(splits):
        block = shape(up_to((stop - begin) * levels, SUBS), LANES)
        blocks = call(
            functools.partial(mix_kernel, plan, sources[s], begin, stop),
            (block,) * group,
            high,
            low,
            *held[s],
            flops=10**9,
        )
        back.append(exchange(blocks))

    result = ()
    for s, tiles in enumerate((range(cut), range(cut, plan.tiles))):
        assert len(tiles) <= cut
        result = (
            pl.pallas_call(
                functools.partial(finish_kernel, plan, *splits[s], tiles),
                grid=(1,),
                out_shape=shape(*increment.shape),
                in_specs=[VMEM] * (group + 1) + [pl.BlockSpec(memory_space=pl.ANY)] * s,
                out_specs=pl.BlockSpec((levels, plan.rows, cut * LANES), lambda _, s=s: (0, 0, s)),
                scratch_shapes=[pltpu.VMEM((cut, levels * plan.rows_held, LANES), f32)],
                input_output_aliases={group + 1: 0} if s else {},
                compiler_params=pltpu.CompilerParams(vmem_limit_bytes=14 << 20),
                cost_estimate=pl.CostEstimate(
                    flops=10**7, bytes_accessed=1 << 20, transcendentals=0
                ),
            )(ground_level, *back[s], *result),
        )
    return result[0]


def solution(mesh):
    return jax.shard_map(
        program,
        mesh=mesh,
        in_specs=(P("lev", "tile", None), P("lev"), P(), P(), P("tile", None)),
        out_specs=P("lev", "tile", None),
        check_vma=False,
    )
```
